512 devices in a mesh: flow: 64 (over y, z), lat: 8 (over x, core).
Axes of the slice: x: 4, y: 8, z: 8, core: 2. Of those that a mesh axis runs over, the one named last changes fastest.
Arguments:
- concentration: float32 [3, 1024, 256, 128], P(None, 'flow', 'lat'), may hold values from 0 to 2
- courant: float32 [3, 1024, 256, 128], P(None, 'flow', 'lat'), may hold values from 500 to 4000
- rates: float32 [2, 1024, 256, 128], P(None, 'flow', 'lat'), may hold values from 0.2 to 3
- spread: float32 [256, 128], P('lat'), may hold values from 0.02 to 0.2
- inlet: float32 [3, 256, 128], P(None, 'lat'), may hold values from 200 to 2000
Outputs:
- fresh: float32 [3, 1024, 256, 128], P(None, 'flow', 'lat')
The draws below stay inside these ranges and needn't reach their ends.
All inputs are finite; a program needn't handle non-finite values.
Results may differ from the reference program's by a relative error of at most 0.000066.
Values sent between devices are 32-bit elements; how exact they have to be, the bound alone decides.
No kernel may reach another device: no remote copies, remote signals or barrier semaphores. Data moves between devices by JAX's collectives and lax.ppermute only.
A program may use at most 64 MiB of HBM per device.

```python
import math
import jax
import jax.numpy as jnp
from jax import lax

NZ = 128
NX = 1024
NY = 256


def block_scale(own_key, extent, pieces, low, top_value):
    def one(dim, blocks):
        heights = jax.random.uniform(jax.random.fold_in(jax.random.fold_in(own_key, 6), dim), (blocks,), jnp.float32, low / len(pieces), top_value / len(pieces))
        return jnp.repeat(jnp.exp(heights), extent[dim] // blocks).reshape((-1,) + (1,) * (len(extent) - dim - 1))

    loudness = one(*pieces[0])
    for cut in pieces[1:]:
        loudness = loudness * one(*cut)
    return loudness


def setup_inputs(seed: int = 0) -> dict:
    streams_of = jax.random.split(jax.random.key(seed), 6)
    return {
        "concentration": jnp.clip(2.0 * jax.random.uniform(streams_of[0], (3, NX, NY, NZ), jnp.float32) ** block_scale(streams_of[0], (3, NX, NY, NZ), ((1, 64), (2, 8)), -0.2, 0.2), 0.0, 2.0),
        "courant": jnp.clip(jnp.exp(math.log(4000.0) - 2.0794415 * jax.random.uniform(streams_of[1], (3, NX, NY, NZ), jnp.float32) ** block_scale(streams_of[1], (3, NX, NY, NZ), ((1, 64), (2, 8)), -0.2, 0.2)), 500.0, 4000.0),
        "rates": jnp.clip(jnp.exp(math.log(3.0) - 2.7080502 * jax.random.uniform(streams_of[2], (2, NX, NY, NZ), jnp.float32) ** block_scale(streams_of[2], (2, NX, NY, NZ), ((1, 64), (2, 8)), -0.2, 0.2)), 0.2, 3.0),
        "spread": jnp.clip(jnp.exp(math.log(0.2) - 2.3025851 * jax.random.uniform(streams_of[3], (NY, NZ), jnp.float32) ** block_scale(streams_of[3], (NY, NZ), ((0, 8),), -0.2, 0.2)), 0.02, 0.2),
        "inlet": jnp.clip(jnp.exp(math.log(2000.0) - 2.3025851 * jax.random.uniform(streams_of[4], (3, NY, NZ), jnp.float32) ** block_scale(streams_of[4], (3, NY, NZ), ((1, 8),), -0.2, 0.2)), 200.0, 2000.0),
    }


def lateral(concentration, spread):
    padded = jnp.pad(concentration, ((0, 0), (0, 0), (1, 1), (1, 1)))
    beside = padded[:, :, 2:, 1:-1] + padded[:, :, :-2, 1:-1]
    beside = beside + padded[:, :, 1:-1, 2:] + padded[:, :, 1:-1, :-2]
    return concentration + spread[None, None] * (beside - 4.0 * concentration)


def reference(concentration, courant, rates, spread, inlet):
    source = lateral(concentration, spread)

    def advance(flux, cell):
        src, cour, rate = cell
        first = (src[0] + flux[0]) / (1.0 + cour[0] + rate[0])
        second = (src[1] + flux[1] + rate[0] * first) / (1.0 + cour[1] + rate[1])
        third = (src[2] + flux[2] + rate[1] * second) / (1.0 + cour[2])
        fresh_cell = jnp.stack([first, second, third])
        return cour * fresh_cell, fresh_cell

    cells = (jnp.moveaxis(source, 1, 0), jnp.moveaxis(courant, 1, 0), jnp.moveaxis(rates, 1, 0))
    _, result = lax.scan(advance, inlet, cells)
    return jnp.moveaxis(result, 0, 1)
```

```python
import functools

import jax
import jax.numpy as jnp
from jax import lax
from jax.experimental import pallas as pl
from jax.experimental.pallas import tpu as pltpu
from jax.sharding import PartitionSpec as P

VMEM = pl.BlockSpec(memory_space=pltpu.VMEM)
SMEM = pl.BlockSpec(memory_space=pltpu.SMEM)
PARAMS = pltpu.CompilerParams(vmem_limit_bytes=16 * 1024 * 1024)
SLOTS = 8


def shifted(value, distance, axis, edge):
    size = value.shape[axis]
    position = lax.broadcasted_iota(jnp.int32, value.shape, axis)
    moved = pltpu.roll(value, distance % size, axis)
    return jnp.where(position == (0 if distance == 1 else size - 1), edge, moved)


def halves(low, high):
    lane = lax.broadcasted_iota(jnp.int32, low.shape, 1)
    half = low.shape[1] // 2
    first = jnp.where(lane < half, low, pltpu.roll(high, half, 1))
    second = jnp.where(lane < half, pltpu.roll(low, half, 1), high)
    return first, second


def maps_kernel(
    core_ref, conc_ref, cour_ref, rate_ref, spread_ref, chip_ref, link_ref, src_ref, inv_ref, out_ref
):
    cells = conc_ref.shape[1]
    rows = conc_ref.shape[2]
    spread = spread_ref[...]
    even = core_ref[0] == 0
    maps = None
    for i in range(cells):
        src = []
        for c in range(3):
            x = conc_ref[c, i]
            chip = chip_ref[pl.ds(c * cells + i, 1), :]
            link = link_ref[pl.ds(c * cells + i, 1), :]
            below = jnp.broadcast_to(jnp.where(even, link, chip), x.shape)
            above = jnp.broadcast_to(jnp.where(even, chip, link), x.shape)
            beside = shifted(x, -1, 0, above) + shifted(x, 1, 0, below)
            beside = beside + shifted(x, -1, 1, 0.0) + shifted(x, 1, 1, 0.0)
            value = x + spread * (beside - 4.0 * x)
            src_ref[c, i] = value
            src.append(value)
        cour = [cour_ref[c, i] for c in range(3)]
        rate = [rate_ref[c, i] for c in range(2)]
        inv = [
            1.0 / (1.0 + cour[0] + rate[0]),
            1.0 / (1.0 + cour[1] + rate[1]),
            1.0 / (1.0 + cour[2]),
        ]
        for c in range(3):
            inv_ref[c, i] = inv[c]
        gain = [cour[c] * inv[c] for c in range(3)]
        if maps is None:
            u0 = inv[0]
            u1 = inv[1] * (rate[0] * u0)
            v1 = inv[1]
            aa = gain[0]
            pa = cour[1] * u1
            pp = gain[1]
            va = gain[2] * (rate[1] * u1)
            vp = gain[2] * (rate[1] * v1)
            vv = gain[2]
            u0 = inv[0] * src[0]
            u1 = inv[1] * (src[1] + rate[0] * u0)
            off_a = cour[0] * u0
            off_p = cour[1] * u1
            off_v = gain[2] * (src[2] + rate[1] * u1)
        else:
            aa, pa, pp, va, vp, vv, off_a, off_p, off_v = maps
            u0 = inv[0] * aa
            u1 = inv[1] * (pa + rate[0] * u0)
            v1 = inv[1] * pp
            aa = cour[0] * u0
            pa = cour[1] * u1
            pp = cour[1] * v1
            va = gain[2] * (va + rate[1] * u1)
            vp = gain[2] * (vp + rate[1] * v1)
            vv = gain[2] * vv
            u0 = inv[0] * (src[0] + off_a)
            u1 = inv[1] * (src[1] + off_p + rate[0] * u0)
            off_a = cour[0] * u0
            off_p = cour[1] * u1
            off_v = gain[2] * (src[2] + off_v + rate[1] * u1)
        maps = (aa, pa, pp, va, vp, vv, off_a, off_p, off_v)
    listed = list(maps)
    listed.append(jnp.zeros_like(spread))
    for j in range(5):
        first, second = halves(listed[2 * j], listed[2 * j + 1])
        out_ref[pl.ds(j, rows, stride=2 * SLOTS), :] = first
        out_ref[pl.ds(SLOTS + j, rows, stride=2 * SLOTS), :] = second
    for j in range(5, SLOTS):
        out_ref[pl.ds(j, rows, stride=2 * SLOTS), :] = listed[-1]
        out_ref[pl.ds(SLOTS + j, rows, stride=2 * SLOTS), :] = listed[-1]


def relay_kernel(place_ref, maps_ref, inlet_ref, out_ref, map_scr, flux_scr):
    count = out_ref.shape[0] // 2
    lanes = out_ref.shape[1]
    half = lanes // 2
    for j in range(5):
        pair = maps_ref[pl.ds(j, count, stride=SLOTS), :]
        map_scr[2 * j] = pair
        if 2 * j + 1 < 9:
            map_scr[2 * j + 1] = pltpu.roll(pair, half, 1)
    place = place_ref[0]
    row = place // 2
    odd = place - 2 * row
    flux = []
    for c in range(3):
        line = inlet_ref[c, pl.ds(row, 1), :]
        flux.append(jnp.where(odd == 1, pltpu.roll(line, half, 1), line))
    for f in range(count):
        for c in range(3):
            flux_scr[c, pl.ds(f, 1), :] = flux[c]
        m = [map_scr[j, pl.ds(f, 1), :] for j in range(9)]
        flux = [
            m[0] * flux[0] + m[6],
            (m[1] * flux[0] + m[7]) + m[2] * flux[1],
            (m[3] * flux[0] + m[8]) + (m[4] * flux[1] + m[5] * flux[2]),
        ]
    lane = lax.broadcasted_iota(jnp.int32, (count, lanes), 1)
    first = jnp.where(lane < half, flux_scr[0], pltpu.roll(flux_scr[1], half, 1))
    out_ref[pl.ds(0, count, stride=2), :] = first
    out_ref[pl.ds(1, count, stride=2), :] = flux_scr[2]


def fresh_kernel(flux_ref, src_ref, inv_ref, cour_ref, rate_ref, out_ref):
    cells, rows, lanes = src_ref.shape[1:]
    half = lanes // 2
    lane = lax.broadcasted_iota(jnp.int32, (rows, lanes), 1)

    def half_row(h, j):
        return flux_ref[pl.ds(2 * h + j, rows, stride=4), :]

    pair_l, pair_h = half_row(0, 0), half_row(1, 0)
    third_l, third_h = half_row(0, 1), half_row(1, 1)
    flux = [
        jnp.where(lane < half, pair_l, pltpu.roll(pair_h, half, 1)),
        jnp.where(lane < half, pltpu.roll(pair_l, half, 1), pair_h),
        jnp.where(lane < half, third_l, pltpu.roll(third_h, half, 1)),
    ]
    for i in range(cells):
        first = inv_ref[0, i] * (src_ref[0, i] + flux[0])
        second = inv_ref[1, i] * (src_ref[1, i] + flux[1] + rate_ref[0, i] * first)
        third = inv_ref[2, i] * (src_ref[2, i] + flux[2] + rate_ref[1, i] * second)
        values = (first, second, third)
        for c in range(3):
            out_ref[c, i] = values[c]
        flux = [cour_ref[c, i] * values[c] for c in range(3)]


def halo(concentration):
    _, cells, rows, lanes = concentration.shape
    count = lax.axis_size("lat")
    core = lax.axis_index("lat") % 2
    low = concentration[:, :, 0, :].reshape(3 * cells, lanes)
    high = concentration[:, :, rows - 1, :].reshape(3 * cells, lanes)
    to_chip = jnp.where(core == 0, high, low)
    to_link = jnp.where(core == 0, low, high)
    links = [(i, i + 1) for i in range(1, count - 1, 2)]
    links = links + [(b, a) for a, b in links]
    link = lax.ppermute(to_link, "lat", links)
    chip = lax.ppermute(to_chip, "lat", [(i, i ^ 1) for i in range(count)])
    return core, chip, link


def per_device(concentration, courant, rates, spread, inlet):
    _, cells, rows, lanes = concentration.shape
    count = lax.axis_size("flow")
    f32 = jnp.float32
    core, chip, link = halo(concentration)
    block = jax.ShapeDtypeStruct(concentration.shape, f32)
    src, inv, maps = pl.pallas_call(
        maps_kernel,
        out_shape=(block, block, jax.ShapeDtypeStruct((count * SLOTS, lanes), f32)),
        in_specs=[SMEM] + [VMEM] * 6,
        out_specs=(VMEM,) * 3,
        compiler_params=PARAMS,
        name="maps",
    )(core.reshape(1), concentration, courant, rates, spread, chip, link)
    maps = lax.all_to_all(maps.reshape(count, SLOTS, lanes), "flow", 0, 0)
    place = lax.axis_index("flow").reshape(1)
    flux = pl.pallas_call(
        relay_kernel,
        out_shape=jax.ShapeDtypeStruct((count * 2, lanes), f32),
        in_specs=[SMEM] + [VMEM] * 2,
        out_specs=VMEM,
        scratch_shapes=[pltpu.VMEM((10, count, lanes), f32), pltpu.VMEM((3, count, lanes), f32)],
        compiler_params=PARAMS,
        name="relay",
    )(place, maps.reshape(count * SLOTS, lanes), inlet)
    flux = lax.all_to_all(flux.reshape(count, 2, lanes), "flow", 0, 0)
    return pl.pallas_call(
        fresh_kernel,
        out_shape=block,
        in_specs=[VMEM] * 5,
        out_specs=VMEM,
        compiler_params=PARAMS,
        name="fresh",
    )(flux.reshape(count * 2, lanes), src, inv, courant, rates)


def solution(mesh):
    in_specs = (
        P(None, "flow", "lat", None),
        P(None, "flow", "lat", None),
        P(None, "flow", "lat", None),
        P("lat", None),
        P(None, "lat", None),
    )
    out_specs = P(None, "flow", "lat", None)
    return jax.shard_map(
        per_device, mesh=mesh, in_specs=in_specs, out_specs=out_specs, check_vma=False
    )
```

```python
import functools

import jax
import jax.numpy as jnp
from jax import lax
from jax.experimental import pallas as pl
from jax.experimental.pallas import tpu as pltpu
from jax.sharding import PartitionSpec as P

VMEM = pl.BlockSpec(memory_space=pltpu.VMEM)
SMEM = pl.BlockSpec(memory_space=pltpu.SMEM)
PARAMS = pltpu.CompilerParams(vmem_limit_bytes=16 * 1024 * 1024)
SLOTS = 8


def in_hbm(value):
    return pltpu.with_memory_space_constraint(value, pltpu.HBM)


def shifted(value, distance, axis, edge):
    size = value.shape[axis]
    position = lax.broadcasted_iota(jnp.int32, value.shape, axis)
    moved = pltpu.roll(value, distance % size, axis)
    return jnp.where(position == (0 if distance == 1 else size - 1), edge, moved)


def halves(low, high):
    lane = lax.broadcasted_iota(jnp.int32, low.shape, 1)
    half = low.shape[1] // 2
    first = jnp.where(lane < half, low, pltpu.roll(high, half, 1))
    second = jnp.where(lane < half, pltpu.roll(low, half, 1), high)
    return first, second


def load_kernel(core_ref, conc_ref, held_ref, link_ref, chip_ref, sems):
    rows = conc_ref.shape[2]
    copies = [pltpu.make_async_copy(conc_ref.at[c], held_ref.at[c], sems.at[c]) for c in range(3)]
    for copy in copies:
        copy.start()
    even = core_ref[0] == 0
    for c in range(3):
        copies[c].wait()
        low = held_ref[c, :, 0, :]
        high = held_ref[c, :, rows - 1, :]
        link_ref[c] = jnp.where(even, low, high)
        chip_ref[c] = jnp.where(even, high, low)


def maps_kernel(
    conc_ref, cour_hbm, rate_hbm, spread_ref, src_ref, inv_ref, maps_ref, cour_ref, rate_ref, sems
):
    cells = conc_ref.shape[1]
    part = cells // 2
    loads = []
    for h in range(2):
        span = pl.ds(h * part, part)
        pair = [
            pltpu.make_async_copy(cour_hbm.at[:, span], cour_ref.at[:, span], sems.at[0, h]),
            pltpu.make_async_copy(rate_hbm.at[:, span], rate_ref.at[:, span], sems.at[1, h]),
        ]
        for copy in pair:
            copy.start()
        loads.append(pair)
    spread = spread_ref[...]
    for i in range(cells):
        for c in range(3):
            x = conc_ref[c, i]
            beside = shifted(x, -1, 0, 0.0) + shifted(x, 1, 0, 0.0)
            beside = beside + shifted(x, -1, 1, 0.0) + shifted(x, 1, 1, 0.0)
            src_ref[c, i] = x + spread * (beside - 4.0 * x)
    maps = None
    for i in range(cells):
        if i % part == 0:
            for copy in loads[i // part]:
                copy.wait()
        src = [src_ref[c, i] for c in range(3)]
        cour = [cour_ref[c, i] for c in range(3)]
        rate = [rate_ref[c, i] for c in range(2)]
        inv = [
            1.0 / (1.0 + cour[0] + rate[0]),
            1.0 / (1.0 + cour[1] + rate[1]),
            1.0 / (1.0 + cour[2]),
        ]
        for c in range(3):
            inv_ref[c, i] = inv[c]
        gain = [cour[c] * inv[c] for c in range(3)]
        if maps is None:
            u0 = inv[0]
            u1 = inv[1] * (rate[0] * u0)
            v1 = inv[1]
            aa = gain[0]
            pa = cour[1] * u1
            pp = gain[1]
            va = gain[2] * (rate[1] * u1)
            vp = gain[2] * (rate[1] * v1)
            vv = gain[2]
            u0 = inv[0] * src[0]
            u1 = inv[1] * (src[1] + rate[0] * u0)
            off_a = cour[0] * u0
            off_p = cour[1] * u1
            off_v = gain[2] * (src[2] + rate[1] * u1)
        else:
            aa, pa, pp, va, vp, vv, off_a, off_p, off_v = maps
            u0 = inv[0] * aa
            u1 = inv[1] * (pa + rate[0] * u0)
            v1 = inv[1] * pp
            aa = cour[0] * u0
            pa = cour[1] * u1
            pp = cour[1] * v1
            va = gain[2] * (va + rate[1] * u1)
            vp = gain[2] * (vp + rate[1] * v1)
            vv = gain[2] * vv
            u0 = inv[0] * (src[0] + off_a)
            u1 = inv[1] * (src[1] + off_p + rate[0] * u0)
            off_a = cour[0] * u0
            off_p = cour[1] * u1
            off_v = gain[2] * (src[2] + off_v + rate[1] * u1)
        maps = (aa, pa, pp, va, vp, vv, off_a, off_p, off_v)
    for j in range(9):
        maps_ref[j] = maps[j]


def seam_kernel(
    core_ref, chip_ref, link_ref, spread_ref, cour_ref, rate_ref, inv_ref, maps_ref, src_in_ref, src_ref, out_ref
):
    cells, rows = src_ref.shape[1:3]
    even = core_ref[0] == 0

    def edge(ref, *index):
        return jnp.concatenate([ref[(*index, pl.ds(0, 8))], ref[(*index, pl.ds(rows - 8, 8))]], axis=0)

    spread = edge(spread_ref)
    line = lax.broadcasted_iota(jnp.int32, spread.shape, 0)
    lower = jnp.where(line == 0, spread, 0.0)
    upper = jnp.where(line == 15, spread, 0.0)
    for_chip = jnp.where(even, upper, lower)
    for_link = jnp.where(even, lower, upper)
    flux = None
    for i in range(cells):
        inv = [edge(inv_ref, c, i) for c in range(3)]
        cour = [edge(cour_ref, c, i) for c in range(3)]
        rate = [edge(rate_ref, c, i) for c in range(2)]
        add = []
        for c in range(3):
            chip = chip_ref[pl.ds(c * cells + i, 1), :]
            link = link_ref[pl.ds(c * cells + i, 1), :]
            value = for_chip * chip + for_link * link
            add.append(value)
            src_ref[c, i, pl.ds(0, 8)] = src_in_ref[c, i, pl.ds(0, 8)] + value[:8]
            src_ref[c, i, pl.ds(rows - 8, 8)] = src_in_ref[c, i, pl.ds(rows - 8, 8)] + value[8:]
        if flux is not None:
            add = [add[c] + flux[c] for c in range(3)]
        u0 = inv[0] * add[0]
        u1 = inv[1] * (add[1] + rate[0] * u0)
        u2 = inv[2] * (add[2] + rate[1] * u1)
        flux = [cour[0] * u0, cour[1] * u1, cour[2] * u2]
    listed = [maps_ref[j] for j in range(9)]
    for c in range(3):
        own = listed[6 + c]
        listed[6 + c] = jnp.concatenate(
            [own[:8] + flux[c][:8], own[8:rows - 8], own[rows - 8:] + flux[c][8:]], axis=0
        )
    zeros = jnp.zeros_like(listed[0])
    listed.append(zeros)
    for j in range(SLOTS):
        first, second = halves(listed[2 * j], listed[2 * j + 1]) if j < 5 else (zeros, zeros)
        out_ref[pl.ds(j, rows, stride=2 * SLOTS), :] = first
        out_ref[pl.ds(SLOTS + j, rows, stride=2 * SLOTS), :] = second


def relay_kernel(place_ref, maps_ref, inlet_ref, out_ref, map_scr, flux_scr):
    count = out_ref.shape[0] // 2
    lanes = out_ref.shape[1]
    half = lanes // 2
    for j in range(5):
        pair = maps_ref[pl.ds(j, count, stride=SLOTS), :]
        map_scr[2 * j] = pair
        if 2 * j + 1 < 9:
            map_scr[2 * j + 1] = pltpu.roll(pair, half, 1)
    place = place_ref[0]
    row = place // 2
    odd = place - 2 * row
    flux = []
    for c in range(3):
        line = inlet_ref[c, pl.ds(row, 1), :]
        flux.append(jnp.where(odd == 1, pltpu.roll(line, half, 1), line))
    for f in range(count):
        for c in range(3):
            flux_scr[c, pl.ds(f, 1), :] = flux[c]
        m = [map_scr[j, pl.ds(f, 1), :] for j in range(9)]
        flux = [
            m[0] * flux[0] + m[6],
            (m[1] * flux[0] + m[7]) + m[2] * flux[1],
            (m[3] * flux[0] + m[8]) + (m[4] * flux[1] + m[5] * flux[2]),
        ]
    lane = lax.broadcasted_iota(jnp.int32, (count, lanes), 1)
    first = jnp.where(lane < half, flux_scr[0], pltpu.roll(flux_scr[1], half, 1))
    out_ref[pl.ds(0, count, stride=2), :] = first
    out_ref[pl.ds(1, count, stride=2), :] = flux_scr[2]


def fresh_kernel(flux_ref, src_ref, inv_ref, cour_ref, rate_ref, out_ref):
    cells, rows, lanes = src_ref.shape[1:]
    half = lanes // 2
    lane = lax.broadcasted_iota(jnp.int32, (rows, lanes), 1)

    def half_row(h, j):
        return flux_ref[pl.ds(2 * h + j, rows, stride=4), :]

    pair_l, pair_h = half_row(0, 0), half_row(1, 0)
    third_l, third_h = half_row(0, 1), half_row(1, 1)
    flux = [
        jnp.where(lane < half, pair_l, pltpu.roll(pair_h, half, 1)),
        jnp.where(lane < half, pltpu.roll(pair_l, half, 1), pair_h),
        jnp.where(lane < half, third_l, pltpu.roll(third_h, half, 1)),
    ]
    for i in range(cells):
        first = inv_ref[0, i] * (src_ref[0, i] + flux[0])
        second = inv_ref[1, i] * (src_ref[1, i] + flux[1] + rate_ref[0, i] * first)
        third = inv_ref[2, i] * (src_ref[2, i] + flux[2] + rate_ref[1, i] * second)
        values = (first, second, third)
        for c in range(3):
            out_ref[c, i] = values[c]
        flux = [cour_ref[c, i] * values[c] for c in range(3)]


def per_device(concentration, courant, rates, spread, inlet):
    _, cells, rows, lanes = concentration.shape
    count = lax.axis_size("flow")
    across = lax.axis_size("lat")
    f32 = jnp.float32
    core = (lax.axis_index("lat") % 2).reshape(1)
    place = lax.axis_index("flow").reshape(1)
    block = jax.ShapeDtypeStruct(concentration.shape, f32)
    lines = jax.ShapeDtypeStruct((3, cells, lanes), f32)
    hbm = pl.BlockSpec(memory_space=pltpu.HBM)
    conc, to_link, to_chip = pl.pallas_call(
        load_kernel,
        out_shape=(block, lines, lines),
        in_specs=[SMEM, hbm],
        out_specs=(VMEM,) * 3,
        scratch_shapes=[pltpu.SemaphoreType.DMA((3,))],
        compiler_params=PARAMS,
        name="load",
    )(core, in_hbm(concentration))
    links = [(i, i + 1) for i in range(1, across - 1, 2)]
    links = links + [(b, a) for a, b in links]
    link = lax.ppermute(to_link.reshape(3 * cells, lanes), "lat", links)
    chip = lax.ppermute(to_chip.reshape(3 * cells, lanes), "lat", [(i, i ^ 1) for i in range(across)])
    src, inv, maps, cour, rate = pl.pallas_call(
        maps_kernel,
        out_shape=(
            block,
            block,
            jax.ShapeDtypeStruct((9, rows, lanes), f32),
            block,
            jax.ShapeDtypeStruct(rates.shape, f32),
        ),
        in_specs=[VMEM, hbm, hbm, VMEM],
        out_specs=(VMEM,) * 5,
        scratch_shapes=[pltpu.SemaphoreType.DMA((2, 2))],
        compiler_params=PARAMS,
        cost_estimate=pl.CostEstimate(flops=0, bytes_accessed=8 * 1024 * 1024, transcendentals=0),
        name="maps",
    )(conc, in_hbm(courant), in_hbm(rates), spread)
    src, packed = pl.pallas_call(
        seam_kernel,
        out_shape=(block, jax.ShapeDtypeStruct((count * SLOTS, lanes), f32)),
        in_specs=[SMEM] + [VMEM] * 8,
        out_specs=(VMEM, VMEM),
        input_output_aliases={8: 0},
        compiler_params=PARAMS,
        name="seam",
    )(core, chip, link, spread, cour, rate, inv, maps, src)
    packed = lax.all_to_all(packed.reshape(count, SLOTS, lanes), "flow", 0, 0)
    flux = pl.pallas_call(
        relay_kernel,
        out_shape=jax.ShapeDtypeStruct((count * 2, lanes), f32),
        in_specs=[SMEM] + [VMEM] * 2,
        out_specs=VMEM,
        scratch_shapes=[pltpu.VMEM((10, count, lanes), f32), pltpu.VMEM((3, count, lanes), f32)],
        compiler_params=PARAMS,
        name="relay",
    )(place, packed.reshape(count * SLOTS, lanes), inlet)
    flux = lax.all_to_all(flux.reshape(count, 2, lanes), "flow", 0, 0)
    return pl.pallas_call(
        fresh_kernel,
        out_shape=block,
        in_specs=[VMEM] * 5,
        out_specs=VMEM,
        compiler_params=PARAMS,
        name="fresh",
    )(flux.reshape(count * 2, lanes), src, inv, cour, rate)


def solution(mesh):
    in_specs = (
        P(None, "flow", "lat", None),
        P(None, "flow", "lat", None),
        P(None, "flow", "lat", None),
        P("lat", None),
        P(None, "lat", None),
    )
    out_specs = P(None, "flow", "lat", None)
    return jax.shard_map(
        per_device, mesh=mesh, in_specs=in_specs, out_specs=out_specs, check_vma=False
    )
```

```python
import functools

import jax
import jax.numpy as jnp
from jax import lax
from jax.experimental import pallas as pl
from jax.experimental.pallas import tpu as pltpu
from jax.sharding import PartitionSpec as P

VMEM = pl.BlockSpec(memory_space=pltpu.VMEM)
SMEM = pl.BlockSpec(memory_space=pltpu.SMEM)
PARAMS = pltpu.CompilerParams(vmem_limit_bytes=16 * 1024 * 1024)
SLOTS = 5


def in_hbm(value):
    return pltpu.with_memory_space_constraint(value, pltpu.HBM)


def in_vmem(value):
    return pltpu.with_memory_space_constraint(value, pltpu.VMEM)


def halves(low, high):
    lane = lax.broadcasted_iota(jnp.int32, low.shape, 1)
    half = low.shape[1] // 2
    first = jnp.where(lane < half, low, pltpu.roll(high, half, 1))
    second = jnp.where(lane < half, pltpu.roll(low, half, 1), high)
    return first, second


def even_core(place_ref):
    return place_ref[0] % 2 == 0


def load_kernel(
    place_ref, conc_ref, spread_hbm, inlet_hbm, held_ref, link_ref, chip_ref, spread_ref, inlet_ref, sems
):
    rows = conc_ref.shape[2]
    copies = [
        pltpu.make_async_copy(conc_ref.at[c], held_ref.at[c], sems.at[c]) for c in range(3)
    ]
    copies.append(pltpu.make_async_copy(spread_hbm, spread_ref, sems.at[3]))
    copies.append(pltpu.make_async_copy(inlet_hbm, inlet_ref, sems.at[4]))
    for copy in copies:
        copy.start()
    even = even_core(place_ref)
    for c in range(3):
        copies[c].wait()
        low = held_ref[c, :, 0, :]
        high = held_ref[c, :, rows - 1, :]
        link_ref[c] = jnp.where(even, low, high)
        chip_ref[c] = jnp.where(even, high, low)
    copies[3].wait()
    copies[4].wait()


def maps_kernel(conc_ref, cour_ref, rate_hbm, spread_ref, src_ref, inv_ref, maps_ref, rate_ref, sems):
    cells = src_ref.shape[1]
    part = cells // sems.shape[0]
    loads = []
    for h in range(sems.shape[0]):
        span = pl.ds(h * part, part)
        loads.append(pltpu.make_async_copy(rate_hbm.at[:, span], rate_ref.at[:, span], sems.at[h]))
        loads[h].start()
    spread = spread_ref[...]
    rows, lanes = spread.shape
    lane = lax.broadcasted_iota(jnp.int32, spread.shape, 1)
    from_left = jnp.where(lane == 0, 0.0, spread)
    from_right = jnp.where(lane == lanes - 1, 0.0, spread)
    row = lax.broadcasted_iota(jnp.int32, spread.shape, 0)
    from_below = jnp.where(row == 0, 0.0, spread)
    from_above = jnp.where(row == rows - 1, 0.0, spread)
    keep = 1.0 - 4.0 * spread
    for i in range(cells):
        for c in range(3):
            x = conc_ref[c, i]
            sides = from_left * pltpu.roll(x, 1, 1) + from_right * pltpu.roll(x, lanes - 1, 1)
            ends = from_below * pltpu.roll(x, 1, 0) + from_above * pltpu.roll(x, rows - 1, 0)
            src_ref[c, i] = keep * x + ends + sides
    maps = None
    for i in range(cells):
        if i % part == 0:
            loads[i // part].wait()
        src = [src_ref[c, i] for c in range(3)]
        cour = [cour_ref[c, i] for c in range(3)]
        rate = [rate_ref[c, i] for c in range(2)]
        under = [1.0 + cour[0] + rate[0], 1.0 + cour[1] + rate[1], 1.0 + cour[2]]
        pair = under[0] * under[1]
        whole = 1.0 / (pair * under[2])
        both = whole * under[2]
        inv = [both * under[1], both * under[0], whole * pair]
        for c in range(3):
            inv_ref[c, i] = inv[c]
        gain = [cour[c] * inv[c] for c in range(3)]
        if maps is None:
            u0 = inv[0]
            u1 = inv[1] * (rate[0] * u0)
            v1 = inv[1]
            aa = gain[0]
            pa = cour[1] * u1
            pp = gain[1]
            va = gain[2] * (rate[1] * u1)
            vp = gain[2] * (rate[1] * v1)
            vv = gain[2]
            u0 = inv[0] * src[0]
            u1 = inv[1] * (src[1] + rate[0] * u0)
            off_a = cour[0] * u0
            off_p = cour[1] * u1
            off_v = gain[2] * (src[2] + rate[1] * u1)
        else:
            aa, pa, pp, va, vp, vv, off_a, off_p, off_v = maps
            u0 = inv[0] * aa
            u1 = inv[1] * (pa + rate[0] * u0)
            v1 = inv[1] * pp
            aa = cour[0] * u0
            pa = cour[1] * u1
            pp = cour[1] * v1
            va = gain[2] * (va + rate[1] * u1)
            vp = gain[2] * (vp + rate[1] * v1)
            vv = gain[2] * vv
            u0 = inv[0] * (src[0] + off_a)
            u1 = inv[1] * (src[1] + off_p + rate[0] * u0)
            off_a = cour[0] * u0
            off_p = cour[1] * u1
            off_v = gain[2] * (src[2] + off_v + rate[1] * u1)
        maps = (aa, pa, pp, va, vp, vv, off_a, off_p, off_v)
    for j in range(9):
        maps_ref[j] = maps[j]


def seam_kernel(
    place_ref, chip_ref, link_ref, spread_ref, cour_ref, rate_ref, inv_ref, maps_ref, src_in_ref, src_ref, out_ref
):
    cells, rows = src_ref.shape[1:3]
    even = even_core(place_ref)

    def edge(ref, *index):
        return jnp.concatenate([ref[(*index, pl.ds(0, 8))], ref[(*index, pl.ds(rows - 8, 8))]], axis=0)

    spread = edge(spread_ref)
    line = lax.broadcasted_iota(jnp.int32, spread.shape, 0)
    lower = jnp.where(line == 0, spread, 0.0)
    upper = jnp.where(line == 15, spread, 0.0)
    for_chip = jnp.where(even, upper, lower)
    for_link = jnp.where(even, lower, upper)
    flux = None
    for i in range(cells):
        inv = [edge(inv_ref, c, i) for c in range(3)]
        cour = [edge(cour_ref, c, i) for c in range(3)]
        rate = [edge(rate_ref, c, i) for c in range(2)]
        add = []
        for c in range(3):
            chip = chip_ref[pl.ds(c * cells + i, 1), :]
            link = link_ref[pl.ds(c * cells + i, 1), :]
            value = for_chip * chip + for_link * link
            add.append(value)
            src_ref[c, i, pl.ds(0, 8)] = src_in_ref[c, i, pl.ds(0, 8)] + value[:8]
            src_ref[c, i, pl.ds(rows - 8, 8)] = src_in_ref[c, i, pl.ds(rows - 8, 8)] + value[8:]
        if flux is not None:
            add = [add[c] + flux[c] for c in range(3)]
        u0 = inv[0] * add[0]
        u1 = inv[1] * (add[1] + rate[0] * u0)
        u2 = inv[2] * (add[2] + rate[1] * u1)
        flux = [cour[0] * u0, cour[1] * u1, cour[2] * u2]
    listed = [maps_ref[j] for j in range(9)]
    for c in range(3):
        own = listed[6 + c]
        listed[6 + c] = jnp.concatenate(
            [own[:8] + flux[c][:8], own[8:rows - 8], own[rows - 8:] + flux[c][8:]], axis=0
        )
    listed.append(listed[8])
    for j in range(SLOTS):
        first, second = halves(listed[2 * j], listed[2 * j + 1])
        out_ref[pl.ds(j, rows, stride=2 * SLOTS), :] = first
        out_ref[pl.ds(SLOTS + j, rows, stride=2 * SLOTS), :] = second


def relay_kernel(place_ref, maps_ref, inlet_ref, out_ref, map_scr, flux_scr):
    count = out_ref.shape[0] // 2
    lanes = out_ref.shape[1]
    half = lanes // 2
    for j in range(5):
        pair = maps_ref[pl.ds(j, count, stride=SLOTS), :]
        map_scr[2 * j] = pair
        if 2 * j + 1 < 9:
            map_scr[2 * j + 1] = pltpu.roll(pair, half, 1)
    place = place_ref[0] // 2
    row = place // 2
    odd = place % 2
    flux = []
    for c in range(3):
        line = inlet_ref[c, pl.ds(row, 1), :]
        flux.append(jnp.where(odd == 1, pltpu.roll(line, half, 1), line))
    for f in range(count):
        for c in range(3):
            flux_scr[c, pl.ds(f, 1), :] = flux[c]
        m = [map_scr[j, pl.ds(f, 1), :] for j in range(9)]
        flux = [
            m[0] * flux[0] + m[6],
            (m[1] * flux[0] + m[7]) + m[2] * flux[1],
            (m[3] * flux[0] + m[8]) + (m[4] * flux[1] + m[5] * flux[2]),
        ]
    lane = lax.broadcasted_iota(jnp.int32, (count, lanes), 1)
    first = jnp.where(lane < half, flux_scr[0], pltpu.roll(flux_scr[1], half, 1))
    out_ref[pl.ds(0, count, stride=2), :] = first
    out_ref[pl.ds(1, count, stride=2), :] = flux_scr[2]


def fresh_kernel(flux_ref, src_ref, inv_ref, cour_ref, rate_ref, out_hbm, out_ref, sems):
    cells, rows, lanes = src_ref.shape[1:]
    half = lanes // 2
    lane = lax.broadcasted_iota(jnp.int32, (rows, lanes), 1)

    def half_row(h, j):
        return flux_ref[pl.ds(2 * h + j, rows, stride=4), :]

    pair_l, pair_h = half_row(0, 0), half_row(1, 0)
    third_l, third_h = half_row(0, 1), half_row(1, 1)
    flux = [
        jnp.where(lane < half, pair_l, pltpu.roll(pair_h, half, 1)),
        jnp.where(lane < half, pltpu.roll(pair_l, half, 1), pair_h),
        jnp.where(lane < half, third_l, pltpu.roll(third_h, half, 1)),
    ]
    part = cells // sems.shape[0]
    copies = []
    for i in range(cells):
        first = inv_ref[0, i] * (src_ref[0, i] + flux[0])
        second = inv_ref[1, i] * (src_ref[1, i] + flux[1] + rate_ref[0, i] * first)
        third = inv_ref[2, i] * (src_ref[2, i] + flux[2] + rate_ref[1, i] * second)
        values = (first, second, third)
        for c in range(3):
            out_ref[c, i] = values[c]
        flux = [cour_ref[c, i] * values[c] for c in range(3)]
        if (i + 1) % part == 0:
            span = pl.ds(i + 1 - part, part)
            copies.append(pltpu.make_async_copy(out_ref.at[:, span], out_hbm.at[:, span], sems.at[i // part]))
            copies[-1].start()
    for copy in copies:
        copy.wait()


def per_device(concentration, courant, rates, spread, inlet):
    _, cells, rows, lanes = concentration.shape
    count = lax.axis_size("flow")
    across = lax.axis_size("lat")
    f32 = jnp.float32
    place = (lax.axis_index("flow") * 2 + lax.axis_index("lat") % 2).reshape(1)
    block = jax.ShapeDtypeStruct(concentration.shape, f32)
    lines = jax.ShapeDtypeStruct((3, cells, lanes), f32)
    hbm = pl.BlockSpec(memory_space=pltpu.HBM)
    conc, to_link, to_chip, spread, inlet = pl.pallas_call(
        load_kernel,
        out_shape=(
            block,
            lines,
            lines,
            jax.ShapeDtypeStruct(spread.shape, f32),
            jax.ShapeDtypeStruct(inlet.shape, f32),
        ),
        in_specs=[SMEM, hbm, hbm, hbm],
        out_specs=(VMEM,) * 5,
        scratch_shapes=[pltpu.SemaphoreType.DMA((5,))],
        compiler_params=PARAMS,
        cost_estimate=pl.CostEstimate(flops=0, bytes_accessed=64 * 1024 * 1024, transcendentals=0),
        name="load",
    )(place, in_hbm(concentration), in_hbm(spread), in_hbm(inlet))
    links = [(i, i + 1) for i in range(1, across - 1, 2)]
    links = links + [(b, a) for a, b in links]
    link = lax.ppermute(to_link.reshape(3 * cells, lanes), "lat", links)
    chip = lax.ppermute(to_chip.reshape(3 * cells, lanes), "lat", [(i, i ^ 1) for i in range(across)])
    cour = in_vmem(courant)
    src, inv, maps, rate = pl.pallas_call(
        maps_kernel,
        out_shape=(
            block,
            block,
            jax.ShapeDtypeStruct((9, rows, lanes), f32),
            jax.ShapeDtypeStruct(rates.shape, f32),
        ),
        in_specs=[VMEM, VMEM, hbm, VMEM],
        out_specs=(VMEM,) * 4,
        scratch_shapes=[pltpu.SemaphoreType.DMA((4,))],
        compiler_params=PARAMS,
        cost_estimate=pl.CostEstimate(flops=0, bytes_accessed=8 * 1024 * 1024, transcendentals=0),
        name="maps",
    )(conc, cour, in_hbm(rates), spread)
    src, packed = pl.pallas_call(
        seam_kernel,
        out_shape=(block, jax.ShapeDtypeStruct((count * SLOTS, lanes), f32)),
        in_specs=[SMEM] + [VMEM] * 8,
        out_specs=(VMEM, VMEM),
        input_output_aliases={8: 0},
        compiler_params=PARAMS,
        name="seam",
    )(place, chip, link, spread, cour, rate, inv, maps, src)
    packed = lax.all_to_all(packed.reshape(count, SLOTS, 1, lanes), "flow", 0, 0)
    flux = pl.pallas_call(
        relay_kernel,
        out_shape=jax.ShapeDtypeStruct((count * 2, lanes), f32),
        in_specs=[SMEM] + [VMEM] * 2,
        out_specs=VMEM,
        scratch_shapes=[pltpu.VMEM((10, count, lanes), f32), pltpu.VMEM((3, count, lanes), f32)],
        compiler_params=PARAMS,
        name="relay",
    )(place, packed.reshape(count * SLOTS, lanes), inlet)
    flux = lax.all_to_all(flux.reshape(count, 2, lanes), "flow", 0, 0)
    return pl.pallas_call(
        fresh_kernel,
        out_shape=block,
        in_specs=[VMEM] * 5,
        out_specs=hbm,
        scratch_shapes=[pltpu.VMEM(block.shape, f32), pltpu.SemaphoreType.DMA((4,))],
        compiler_params=PARAMS,
        name="fresh",
    )(flux.reshape(count * 2, lanes), src, inv, cour, rate)


def solution(mesh):
    in_specs = (
        P(None, "flow", "lat", None),
        P(None, "flow", "lat", None),
        P(None, "flow", "lat", None),
        P("lat", None),
        P(None, "lat", None),
    )
    out_specs = P(None, "flow", "lat", None)
    return jax.shard_map(
        per_device, mesh=mesh, in_specs=in_specs, out_specs=out_specs, check_vma=False
    )
```

```python
import functools

import jax
import jax.numpy as jnp
from jax import lax
from jax.experimental import pallas as pl
from jax.experimental.pallas import tpu as pltpu
from jax.sharding import PartitionSpec as P

VMEM = pl.BlockSpec(memory_space=pltpu.VMEM)
SMEM = pl.BlockSpec(memory_space=pltpu.SMEM)
PARAMS = pltpu.CompilerParams(vmem_limit_bytes=16 * 1024 * 1024)
SLOTS = 5


def in_hbm(value):
    return pltpu.with_memory_space_constraint(value, pltpu.HBM)


def in_vmem(value):
    return pltpu.with_memory_space_constraint(value, pltpu.VMEM)


def halves(low, high):
    lane = lax.broadcasted_iota(jnp.int32, low.shape, 1)
    half = low.shape[1] // 2
    first = jnp.where(lane < half, low, pltpu.roll(high, half, 1))
    second = jnp.where(lane < half, pltpu.roll(low, half, 1), high)
    return first, second


def even_core(place_ref):
    return place_ref[0] % 2 == 0


def load_kernel(
    place_ref,
    conc_hbm,
    rate_hbm,
    spread_hbm,
    inlet_hbm,
    conc_ref,
    link_ref,
    chip_ref,
    rate_ref,
    spread_ref,
    inlet_ref,
    sems,
):
    rows = conc_hbm.shape[2]
    edges = [pltpu.make_async_copy(conc_hbm.at[c], conc_ref.at[c], sems.at[c]) for c in range(3)]
    others = [
        pltpu.make_async_copy(rate_hbm, rate_ref, sems.at[3]),
        pltpu.make_async_copy(spread_hbm, spread_ref, sems.at[4]),
        pltpu.make_async_copy(inlet_hbm, inlet_ref, sems.at[5]),
    ]
    for copy in edges + others:
        copy.start()
    even = even_core(place_ref)
    for c in range(3):
        edges[c].wait()
        low = conc_ref[c, :, 0, :]
        high = conc_ref[c, :, rows - 1, :]
        link_ref[c] = jnp.where(even, low, high)
        chip_ref[c] = jnp.where(even, high, low)
    for copy in others:
        copy.wait()


def maps_kernel(conc_ref, cour_ref, rate_ref, spread_ref, src_ref, inv_ref, maps_ref):
    cells = src_ref.shape[1]
    spread = spread_ref[...]
    rows, lanes = spread.shape
    lane = lax.broadcasted_iota(jnp.int32, spread.shape, 1)
    from_left = jnp.where(lane == 0, 0.0, spread)
    from_right = jnp.where(lane == lanes - 1, 0.0, spread)
    row = lax.broadcasted_iota(jnp.int32, spread.shape, 0)
    from_below = jnp.where(row == 0, 0.0, spread)
    from_above = jnp.where(row == rows - 1, 0.0, spread)
    keep = 1.0 - 4.0 * spread
    for i in range(cells):
        for c in range(3):
            x = conc_ref[c, i]
            sides = from_left * pltpu.roll(x, 1, 1) + from_right * pltpu.roll(x, lanes - 1, 1)
            ends = from_below * pltpu.roll(x, 1, 0) + from_above * pltpu.roll(x, rows - 1, 0)
            src_ref[c, i] = keep * x + ends + sides
    maps = None
    for i in range(cells):
        src = [src_ref[c, i] for c in range(3)]
        cour = [cour_ref[c, i] for c in range(3)]
        rate = [rate_ref[c, i] for c in range(2)]
        under = [1.0 + cour[0] + rate[0], 1.0 + cour[1] + rate[1], 1.0 + cour[2]]
        pair = under[0] * under[1]
        whole = 1.0 / (pair * under[2])
        both = whole * under[2]
        inv = [both * under[1], both * under[0], whole * pair]
        for c in range(3):
            inv_ref[c, i] = inv[c]
        gain = [cour[c] * inv[c] for c in range(3)]
        if maps is None:
            u0 = inv[0]
            u1 = inv[1] * (rate[0] * u0)
            v1 = inv[1]
            aa = gain[0]
            pa = cour[1] * u1
            pp = gain[1]
            va = gain[2] * (rate[1] * u1)
            vp = gain[2] * (rate[1] * v1)
            vv = gain[2]
            u0 = inv[0] * src[0]
            u1 = inv[1] * (src[1] + rate[0] * u0)
            off_a = cour[0] * u0
            off_p = cour[1] * u1
            off_v = gain[2] * (src[2] + rate[1] * u1)
        else:
            aa, pa, pp, va, vp, vv, off_a, off_p, off_v = maps
            u0 = inv[0] * aa
            u1 = inv[1] * (pa + rate[0] * u0)
            v1 = inv[1] * pp
            aa = cour[0] * u0
            pa = cour[1] * u1
            pp = cour[1] * v1
            va = gain[2] * (va + rate[1] * u1)
            vp = gain[2] * (vp + rate[1] * v1)
            vv = gain[2] * vv
            u0 = inv[0] * (src[0] + off_a)
            u1 = inv[1] * (src[1] + off_p + rate[0] * u0)
            off_a = cour[0] * u0
            off_p = cour[1] * u1
            off_v = gain[2] * (src[2] + off_v + rate[1] * u1)
        maps = (aa, pa, pp, va, vp, vv, off_a, off_p, off_v)
    for j in range(9):
        maps_ref[j] = maps[j]


def seam_kernel(
    place_ref, chip_ref, link_ref, spread_ref, cour_ref, rate_ref, inv_ref, maps_ref, src_in_ref, src_ref, out_ref
):
    cells, rows = src_ref.shape[1:3]
    even = even_core(place_ref)

    def edge(ref, *index):
        return jnp.concatenate([ref[(*index, pl.ds(0, 8))], ref[(*index, pl.ds(rows - 8, 8))]], axis=0)

    spread = edge(spread_ref)
    line = lax.broadcasted_iota(jnp.int32, spread.shape, 0)
    lower = jnp.where(line == 0, spread, 0.0)
    upper = jnp.where(line == 15, spread, 0.0)
    for_chip = jnp.where(even, upper, lower)
    for_link = jnp.where(even, lower, upper)
    flux = None
    for i in range(cells):
        inv = [edge(inv_ref, c, i) for c in range(3)]
        cour = [edge(cour_ref, c, i) for c in range(3)]
        rate = [edge(rate_ref, c, i) for c in range(2)]
        add = []
        for c in range(3):
            chip = chip_ref[pl.ds(c * cells + i, 1), :]
            link = link_ref[pl.ds(c * cells + i, 1), :]
            value = for_chip * chip + for_link * link
            add.append(value)
            src_ref[c, i, pl.ds(0, 8)] = src_in_ref[c, i, pl.ds(0, 8)] + value[:8]
            src_ref[c, i, pl.ds(rows - 8, 8)] = src_in_ref[c, i, pl.ds(rows - 8, 8)] + value[8:]
        if flux is not None:
            add = [add[c] + flux[c] for c in range(3)]
        u0 = inv[0] * add[0]
        u1 = inv[1] * (add[1] + rate[0] * u0)
        u2 = inv[2] * (add[2] + rate[1] * u1)
        flux = [cour[0] * u0, cour[1] * u1, cour[2] * u2]
    listed = [maps_ref[j] for j in range(9)]
    for c in range(3):
        own = listed[6 + c]
        listed[6 + c] = jnp.concatenate(
            [own[:8] + flux[c][:8], own[8:rows - 8], own[rows - 8:] + flux[c][8:]], axis=0
        )
    listed.append(listed[8])
    for j in range(SLOTS):
        first, second = halves(listed[2 * j], listed[2 * j + 1])
        out_ref[pl.ds(j, rows, stride=2 * SLOTS), :] = first
        out_ref[pl.ds(SLOTS + j, rows, stride=2 * SLOTS), :] = second


def relay_kernel(place_ref, maps_ref, inlet_ref, out_ref, map_scr, flux_scr):
    count = out_ref.shape[0] // 2
    lanes = out_ref.shape[1]
    half = lanes // 2
    for j in range(5):
        pair = maps_ref[pl.ds(j, count, stride=SLOTS), :]
        map_scr[2 * j] = pair
        if 2 * j + 1 < 9:
            map_scr[2 * j + 1] = pltpu.roll(pair, half, 1)
    place = place_ref[0] // 2
    row = place // 2
    odd = place % 2
    flux = []
    for c in range(3):
        line = inlet_ref[c, pl.ds(row, 1), :]
        flux.append(jnp.where(odd == 1, pltpu.roll(line, half, 1), line))
    for f in range(count):
        for c in range(3):
            flux_scr[c, pl.ds(f, 1), :] = flux[c]
        m = [map_scr[j, pl.ds(f, 1), :] for j in range(9)]
        flux = [
            m[0] * flux[0] + m[6],
            (m[1] * flux[0] + m[7]) + m[2] * flux[1],
            (m[3] * flux[0] + m[8]) + (m[4] * flux[1] + m[5] * flux[2]),
        ]
    lane = lax.broadcasted_iota(jnp.int32, (count, lanes), 1)
    first = jnp.where(lane < half, flux_scr[0], pltpu.roll(flux_scr[1], half, 1))
    out_ref[pl.ds(0, count, stride=2), :] = first
    out_ref[pl.ds(1, count, stride=2), :] = flux_scr[2]


def fresh_kernel(flux_ref, src_ref, inv_ref, cour_ref, rate_ref, out_hbm, out_ref, sems):
    cells, rows, lanes = src_ref.shape[1:]
    half = lanes // 2
    lane = lax.broadcasted_iota(jnp.int32, (rows, lanes), 1)

    def half_row(h, j):
        return flux_ref[pl.ds(2 * h + j, rows, stride=4), :]

    pair_l, pair_h = half_row(0, 0), half_row(1, 0)
    third_l, third_h = half_row(0, 1), half_row(1, 1)
    flux = [
        jnp.where(lane < half, pair_l, pltpu.roll(pair_h, half, 1)),
        jnp.where(lane < half, pltpu.roll(pair_l, half, 1), pair_h),
        jnp.where(lane < half, third_l, pltpu.roll(third_h, half, 1)),
    ]
    part = cells // sems.shape[0]
    copies = []
    for i in range(cells):
        first = inv_ref[0, i] * (src_ref[0, i] + flux[0])
        second = inv_ref[1, i] * (src_ref[1, i] + flux[1] + rate_ref[0, i] * first)
        third = inv_ref[2, i] * (src_ref[2, i] + flux[2] + rate_ref[1, i] * second)
        values = (first, second, third)
        for c in range(3):
            out_ref[c, i] = values[c]
        flux = [cour_ref[c, i] * values[c] for c in range(3)]
        if (i + 1) % part == 0:
            span = pl.ds(i + 1 - part, part)
            copies.append(pltpu.make_async_copy(out_ref.at[:, span], out_hbm.at[:, span], sems.at[i // part]))
            copies[-1].start()
    for copy in copies:
        copy.wait()


def per_device(concentration, courant, rates, spread, inlet):
    _, cells, rows, lanes = concentration.shape
    count = lax.axis_size("flow")
    across = lax.axis_size("lat")
    f32 = jnp.float32
    place = (lax.axis_index("flow") * 2 + lax.axis_index("lat") % 2).reshape(1)
    block = jax.ShapeDtypeStruct(concentration.shape, f32)
    lines = jax.ShapeDtypeStruct((3, cells, lanes), f32)
    hbm = pl.BlockSpec(memory_space=pltpu.HBM)
    conc, to_link, to_chip, rate, spread, inlet = pl.pallas_call(
        load_kernel,
        out_shape=(
            block,
            lines,
            lines,
            jax.ShapeDtypeStruct(rates.shape, f32),
            jax.ShapeDtypeStruct(spread.shape, f32),
            jax.ShapeDtypeStruct(inlet.shape, f32),
        ),
        in_specs=[SMEM] + [hbm] * 4,
        out_specs=(VMEM,) * 6,
        scratch_shapes=[pltpu.SemaphoreType.DMA((6,))],
        compiler_params=PARAMS,
        cost_estimate=pl.CostEstimate(flops=0, bytes_accessed=64 * 1024 * 1024, transcendentals=0),
        name="load",
    )(place, in_hbm(concentration), in_hbm(rates), in_hbm(spread), in_hbm(inlet))
    links = [(i, i + 1) for i in range(1, across - 1, 2)]
    links = links + [(b, a) for a, b in links]
    link = lax.ppermute(to_link.reshape(3 * cells, lanes), "lat", links)
    chip = lax.ppermute(to_chip.reshape(3 * cells, lanes), "lat", [(i, i ^ 1) for i in range(across)])
    cour = in_vmem(courant)
    src, inv, maps = pl.pallas_call(
        maps_kernel,
        out_shape=(
            block,
            block,
            jax.ShapeDtypeStruct((9, rows, lanes), f32),
        ),
        in_specs=[VMEM] * 4,
        out_specs=(VMEM,) * 3,
        compiler_params=PARAMS,
        cost_estimate=pl.CostEstimate(flops=0, bytes_accessed=8 * 1024 * 1024, transcendentals=0),
        name="maps",
    )(conc, cour, rate, spread)
    src, packed = pl.pallas_call(
        seam_kernel,
        out_shape=(block, jax.ShapeDtypeStruct((count * SLOTS, lanes), f32)),
        in_specs=[SMEM] + [VMEM] * 8,
        out_specs=(VMEM, VMEM),
        input_output_aliases={8: 0},
        compiler_params=PARAMS,
        name="seam",
    )(place, chip, link, spread, cour, rate, inv, maps, src)
    packed = lax.all_to_all(packed.reshape(count, SLOTS, 1, lanes), "flow", 0, 0)
    flux = pl.pallas_call(
        relay_kernel,
        out_shape=jax.ShapeDtypeStruct((count * 2, lanes), f32),
        in_specs=[SMEM] + [VMEM] * 2,
        out_specs=VMEM,
        scratch_shapes=[pltpu.VMEM((10, count, lanes), f32), pltpu.VMEM((3, count, lanes), f32)],
        compiler_params=PARAMS,
        name="relay",
    )(place, packed.reshape(count * SLOTS, lanes), inlet)
    flux = lax.all_to_all(flux.reshape(count, 2, lanes), "flow", 0, 0)
    return pl.pallas_call(
        fresh_kernel,
        out_shape=block,
        in_specs=[VMEM] * 5,
        out_specs=hbm,
        scratch_shapes=[pltpu.VMEM(block.shape, f32), pltpu.SemaphoreType.DMA((4,))],
        compiler_params=PARAMS,
        name="fresh",
    )(flux.reshape(count * 2, lanes), src, inv, cour, rate)


def solution(mesh):
    in_specs = (
        P(None, "flow", "lat", None),
        P(None, "flow", "lat", None),
        P(None, "flow", "lat", None),
        P("lat", None),
        P(None, "lat", None),
    )
    out_specs = P(None, "flow", "lat", None)
    return jax.shard_map(
        per_device, mesh=mesh, in_specs=in_specs, out_specs=out_specs, check_vma=False
    )
```

```python
import functools

import jax
import jax.numpy as jnp
from jax import lax
from jax.experimental import pallas as pl
from jax.experimental.pallas import tpu as pltpu
from jax.sharding import PartitionSpec as P

VMEM = pl.BlockSpec(memory_space=pltpu.VMEM)
SMEM = pl.BlockSpec(memory_space=pltpu.SMEM)
PARAMS = pltpu.CompilerParams(vmem_limit_bytes=16 * 1024 * 1024)
SLOTS = 5


def in_hbm(value):
    return pltpu.with_memory_space_constraint(value, pltpu.HBM)


def in_vmem(value):
    return pltpu.with_memory_space_constraint(value, pltpu.VMEM)


def halves(low, high):
    lane = lax.broadcasted_iota(jnp.int32, low.shape, 1)
    half = low.shape[1] // 2
    first = jnp.where(lane < half, low, pltpu.roll(high, half, 1))
    second = jnp.where(lane < half, pltpu.roll(low, half, 1), high)
    return first, second


def load_kernel(
    conc_hbm,
    rate_hbm,
    spread_hbm,
    inlet_hbm,
    conc_ref,
    low_ref,
    high_ref,
    rate_ref,
    spread_ref,
    inlet_ref,
    sems,
):
    rows = conc_hbm.shape[2]
    edges = [pltpu.make_async_copy(conc_hbm.at[c], conc_ref.at[c], sems.at[c]) for c in range(3)]
    others = [
        pltpu.make_async_copy(rate_hbm, rate_ref, sems.at[3]),
        pltpu.make_async_copy(spread_hbm, spread_ref, sems.at[4]),
        pltpu.make_async_copy(inlet_hbm, inlet_ref, sems.at[5]),
    ]
    for copy in edges + others:
        copy.start()
    for c in range(3):
        edges[c].wait()
        low_ref[c] = conc_ref[c, :, 0, :]
        high_ref[c] = conc_ref[c, :, rows - 1, :]
    for copy in others:
        copy.wait()


def maps_kernel(conc_ref, cour_ref, rate_ref, spread_ref, src_ref, inv_ref, maps_ref):
    cells = src_ref.shape[1]
    spread = spread_ref[...]
    rows, lanes = spread.shape
    lane = lax.broadcasted_iota(jnp.int32, spread.shape, 1)
    from_left = jnp.where(lane == 0, 0.0, spread)
    from_right = jnp.where(lane == lanes - 1, 0.0, spread)
    row = lax.broadcasted_iota(jnp.int32, spread.shape, 0)
    from_below = jnp.where(row == 0, 0.0, spread)
    from_above = jnp.where(row == rows - 1, 0.0, spread)
    keep = 1.0 - 4.0 * spread
    for i in range(cells):
        for c in range(3):
            x = conc_ref[c, i]
            sides = from_left * pltpu.roll(x, 1, 1) + from_right * pltpu.roll(x, lanes - 1, 1)
            ends = from_below * pltpu.roll(x, 1, 0) + from_above * pltpu.roll(x, rows - 1, 0)
            src_ref[c, i] = keep * x + ends + sides
    maps = None
    for i in range(cells):
        src = [src_ref[c, i] for c in range(3)]
        cour = [cour_ref[c, i] for c in range(3)]
        rate = [rate_ref[c, i] for c in range(2)]
        under = [1.0 + cour[0] + rate[0], 1.0 + cour[1] + rate[1], 1.0 + cour[2]]
        pair = under[0] * under[1]
        whole = 1.0 / (pair * under[2])
        both = whole * under[2]
        inv = [both * under[1], both * under[0], whole * pair]
        for c in range(3):
            inv_ref[c, i] = inv[c]
        gain = [cour[c] * inv[c] for c in range(3)]
        if maps is None:
            u0 = inv[0]
            u1 = inv[1] * (rate[0] * u0)
            v1 = inv[1]
            aa = gain[0]
            pa = cour[1] * u1
            pp = gain[1]
            va = gain[2] * (rate[1] * u1)
            vp = gain[2] * (rate[1] * v1)
            vv = gain[2]
            u0 = inv[0] * src[0]
            u1 = inv[1] * (src[1] + rate[0] * u0)
            off_a = cour[0] * u0
            off_p = cour[1] * u1
            off_v = gain[2] * (src[2] + rate[1] * u1)
        else:
            aa, pa, pp, va, vp, vv, off_a, off_p, off_v = maps
            u0 = inv[0] * aa
            u1 = inv[1] * (pa + rate[0] * u0)
            v1 = inv[1] * pp
            aa = cour[0] * u0
            pa = cour[1] * u1
            pp = cour[1] * v1
            va = gain[2] * (va + rate[1] * u1)
            vp = gain[2] * (vp + rate[1] * v1)
            vv = gain[2] * vv
            u0 = inv[0] * (src[0] + off_a)
            u1 = inv[1] * (src[1] + off_p + rate[0] * u0)
            off_a = cour[0] * u0
            off_p = cour[1] * u1
            off_v = gain[2] * (src[2] + off_v + rate[1] * u1)
        maps = (aa, pa, pp, va, vp, vv, off_a, off_p, off_v)
    for j in range(9):
        maps_ref[j] = maps[j]


def seam_kernel(
    across, place_ref, below_ref, above_ref, spread_ref, cour_ref, rate_ref, inv_ref, maps_ref, src_in_ref, src_ref, out_ref
):
    cells, rows = src_ref.shape[1:3]
    side = place_ref[0] % across

    def edge(ref, *index):
        return jnp.concatenate([ref[(*index, pl.ds(0, 8))], ref[(*index, pl.ds(rows - 8, 8))]], axis=0)

    spread = edge(spread_ref)
    line = lax.broadcasted_iota(jnp.int32, spread.shape, 0)
    from_below = jnp.where(jnp.logical_and(line == 0, side > 0), spread, 0.0)
    from_above = jnp.where(jnp.logical_and(line == 15, side < across - 1), spread, 0.0)
    flux = None
    for i in range(cells):
        inv = [edge(inv_ref, c, i) for c in range(3)]
        cour = [edge(cour_ref, c, i) for c in range(3)]
        rate = [edge(rate_ref, c, i) for c in range(2)]
        add = []
        for c in range(3):
            below = below_ref[pl.ds(c * cells + i, 1), :]
            above = above_ref[pl.ds(c * cells + i, 1), :]
            value = from_below * below + from_above * above
            add.append(value)
            src_ref[c, i, pl.ds(0, 8)] = src_in_ref[c, i, pl.ds(0, 8)] + value[:8]
            src_ref[c, i, pl.ds(rows - 8, 8)] = src_in_ref[c, i, pl.ds(rows - 8, 8)] + value[8:]
        if flux is not None:
            add = [add[c] + flux[c] for c in range(3)]
        u0 = inv[0] * add[0]
        u1 = inv[1] * (add[1] + rate[0] * u0)
        u2 = inv[2] * (add[2] + rate[1] * u1)
        flux = [cour[0] * u0, cour[1] * u1, cour[2] * u2]
    listed = [maps_ref[j] for j in range(9)]
    for c in range(3):
        own = listed[6 + c]
        listed[6 + c] = jnp.concatenate(
            [own[:8] + flux[c][:8], own[8:rows - 8], own[rows - 8:] + flux[c][8:]], axis=0
        )
    listed.append(listed[8])
    for j in range(SLOTS):
        first, second = halves(listed[2 * j], listed[2 * j + 1])
        out_ref[pl.ds(j, rows, stride=2 * SLOTS), :] = first
        out_ref[pl.ds(SLOTS + j, rows, stride=2 * SLOTS), :] = second


def relay_kernel(across, place_ref, maps_ref, inlet_ref, out_ref, map_scr, flux_scr):
    count = out_ref.shape[0] // 2
    lanes = out_ref.shape[1]
    half = lanes // 2
    for j in range(5):
        pair = maps_ref[pl.ds(j, count, stride=SLOTS), :]
        map_scr[2 * j] = pair
        if 2 * j + 1 < 9:
            map_scr[2 * j + 1] = pltpu.roll(pair, half, 1)
    place = place_ref[0] // across
    row = place // 2
    odd = place % 2
    flux = []
    for c in range(3):
        line = inlet_ref[c, pl.ds(row, 1), :]
        flux.append(jnp.where(odd == 1, pltpu.roll(line, half, 1), line))
    for f in range(count):
        for c in range(3):
            flux_scr[c, pl.ds(f, 1), :] = flux[c]
        m = [map_scr[j, pl.ds(f, 1), :] for j in range(9)]
        flux = [
            m[0] * flux[0] + m[6],
            (m[1] * flux[0] + m[7]) + m[2] * flux[1],
            (m[3] * flux[0] + m[8]) + (m[4] * flux[1] + m[5] * flux[2]),
        ]
    lane = lax.broadcasted_iota(jnp.int32, (count, lanes), 1)
    first = jnp.where(lane < half, flux_scr[0], pltpu.roll(flux_scr[1], half, 1))
    out_ref[pl.ds(0, count, stride=2), :] = first
    out_ref[pl.ds(1, count, stride=2), :] = flux_scr[2]


def fresh_kernel(flux_ref, src_ref, inv_ref, cour_ref, rate_ref, out_hbm, out_ref, sems):
    cells, rows, lanes = src_ref.shape[1:]
    half = lanes // 2
    lane = lax.broadcasted_iota(jnp.int32, (rows, lanes), 1)

    def half_row(h, j):
        return flux_ref[pl.ds(2 * h + j, rows, stride=4), :]

    pair_l, pair_h = half_row(0, 0), half_row(1, 0)
    third_l, third_h = half_row(0, 1), half_row(1, 1)
    flux = [
        jnp.where(lane < half, pair_l, pltpu.roll(pair_h, half, 1)),
        jnp.where(lane < half, pltpu.roll(pair_l, half, 1), pair_h),
        jnp.where(lane < half, third_l, pltpu.roll(third_h, half, 1)),
    ]
    part = cells // sems.shape[0]
    copies = []
    for i in range(cells):
        first = inv_ref[0, i] * (src_ref[0, i] + flux[0])
        second = inv_ref[1, i] * (src_ref[1, i] + flux[1] + rate_ref[0, i] * first)
        third = inv_ref[2, i] * (src_ref[2, i] + flux[2] + rate_ref[1, i] * second)
        values = (first, second, third)
        for c in range(3):
            out_ref[c, i] = values[c]
        flux = [cour_ref[c, i] * values[c] for c in range(3)]
        if (i + 1) % part == 0:
            span = pl.ds(i + 1 - part, part)
            copies.append(pltpu.make_async_copy(out_ref.at[:, span], out_hbm.at[:, span], sems.at[i // part]))
            copies[-1].start()
    for copy in copies:
        copy.wait()


def per_device(concentration, courant, rates, spread, inlet):
    _, cells, rows, lanes = concentration.shape
    count = lax.axis_size("flow")
    across = lax.axis_size("lat")
    f32 = jnp.float32
    place = (lax.axis_index("flow") * across + lax.axis_index("lat")).reshape(1)
    block = jax.ShapeDtypeStruct(concentration.shape, f32)
    lines = jax.ShapeDtypeStruct((3, cells, lanes), f32)
    hbm = pl.BlockSpec(memory_space=pltpu.HBM)
    conc, low, high, rate, spread, inlet = pl.pallas_call(
        load_kernel,
        out_shape=(
            block,
            lines,
            lines,
            jax.ShapeDtypeStruct(rates.shape, f32),
            jax.ShapeDtypeStruct(spread.shape, f32),
            jax.ShapeDtypeStruct(inlet.shape, f32),
        ),
        in_specs=[hbm] * 4,
        out_specs=(VMEM,) * 6,
        scratch_shapes=[pltpu.SemaphoreType.DMA((6,))],
        compiler_params=PARAMS,
        cost_estimate=pl.CostEstimate(flops=0, bytes_accessed=64 * 1024 * 1024, transcendentals=0),
        name="load",
    )(in_hbm(concentration), in_hbm(rates), in_hbm(spread), in_hbm(inlet))
    ring = [(i, (i + 1) % across) for i in range(across)]
    below = lax.ppermute(high.reshape(3 * cells, lanes), "lat", ring)
    above = lax.ppermute(low.reshape(3 * cells, lanes), "lat", [(b, a) for a, b in ring])
    cour = in_vmem(courant)
    src, inv, maps = pl.pallas_call(
        maps_kernel,
        out_shape=(
            block,
            block,
            jax.ShapeDtypeStruct((9, rows, lanes), f32),
        ),
        in_specs=[VMEM] * 4,
        out_specs=(VMEM,) * 3,
        compiler_params=PARAMS,
        cost_estimate=pl.CostEstimate(flops=0, bytes_accessed=8 * 1024 * 1024, transcendentals=0),
        name="maps",
    )(conc, cour, rate, spread)
    src, packed = pl.pallas_call(
        functools.partial(seam_kernel, across),
        out_shape=(block, jax.ShapeDtypeStruct((count * SLOTS, lanes), f32)),
        in_specs=[SMEM] + [VMEM] * 8,
        out_specs=(VMEM, VMEM),
        input_output_aliases={8: 0},
        compiler_params=PARAMS,
        name="seam",
    )(place, below, above, spread, cour, rate, inv, maps, src)
    packed = lax.all_to_all(packed.reshape(count, SLOTS, 1, lanes), "flow", 0, 0)
    flux = pl.pallas_call(
        functools.partial(relay_kernel, across),
        out_shape=jax.ShapeDtypeStruct((count * 2, lanes), f32),
        in_specs=[SMEM] + [VMEM] * 2,
        out_specs=VMEM,
        scratch_shapes=[pltpu.VMEM((10, count, lanes), f32), pltpu.VMEM((3, count, lanes), f32)],
        compiler_params=PARAMS,
        name="relay",
    )(place, packed.reshape(count * SLOTS, lanes), inlet)
    flux = lax.all_to_all(flux.reshape(count, 2, lanes), "flow", 0, 0)
    return pl.pallas_call(
        fresh_kernel,
        out_shape=block,
        in_specs=[VMEM] * 5,
        out_specs=hbm,
        scratch_shapes=[pltpu.VMEM(block.shape, f32), pltpu.SemaphoreType.DMA((4,))],
        compiler_params=PARAMS,
        name="fresh",
    )(flux.reshape(count * 2, lanes), src, inv, cour, rate)


def solution(mesh):
    in_specs = (
        P(None, "flow", "lat", None),
        P(None, "flow", "lat", None),
        P(None, "flow", "lat", None),
        P("lat", None),
        P(None, "lat", None),
    )
    out_specs = P(None, "flow", "lat", None)
    return jax.shard_map(
        per_device, mesh=mesh, in_specs=in_specs, out_specs=out_specs, check_vma=False
    )
```

```python
import functools

import jax
import jax.numpy as jnp
from jax import lax
from jax.experimental import pallas as pl
from jax.experimental.pallas import tpu as pltpu
from jax.sharding import PartitionSpec as P

VMEM = pl.BlockSpec(memory_space=pltpu.VMEM)
SMEM = pl.BlockSpec(memory_space=pltpu.SMEM)
PARAMS = pltpu.CompilerParams(vmem_limit_bytes=16 * 1024 * 1024)
SLOTS = 5


def in_hbm(value):
    return pltpu.with_memory_space_constraint(value, pltpu.HBM)


def in_vmem(value):
    return pltpu.with_memory_space_constraint(value, pltpu.VMEM)


def halves(low, high):
    lane = lax.broadcasted_iota(jnp.int32, low.shape, 1)
    half = low.shape[1] // 2
    first = jnp.where(lane < half, low, pltpu.roll(high, half, 1))
    second = jnp.where(lane < half, pltpu.roll(low, half, 1), high)
    return first, second


def load_kernel(
    conc_hbm,
    rate_hbm,
    spread_hbm,
    inlet_hbm,
    conc_ref,
    low_ref,
    high_ref,
    rate_ref,
    spread_ref,
    inlet_ref,
    sems,
):
    rows = conc_hbm.shape[2]
    edges = [pltpu.make_async_copy(conc_hbm.at[c], conc_ref.at[c], sems.at[c]) for c in range(3)]
    others = [
        pltpu.make_async_copy(rate_hbm, rate_ref, sems.at[3]),
        pltpu.make_async_copy(spread_hbm, spread_ref, sems.at[4]),
        pltpu.make_async_copy(inlet_hbm, inlet_ref, sems.at[5]),
    ]
    for copy in edges + others:
        copy.start()
    for c in range(3):
        edges[c].wait()
        low_ref[c] = conc_ref[c, :, 0, :]
        high_ref[c] = conc_ref[c, :, rows - 1, :]
    for copy in others:
        copy.wait()


def maps_kernel(conc_ref, cour_ref, rate_ref, spread_ref, src_ref, inv_ref, maps_ref):
    cells = src_ref.shape[1]
    spread = spread_ref[...]
    rows, lanes = spread.shape
    lane = lax.broadcasted_iota(jnp.int32, spread.shape, 1)
    from_left = jnp.where(lane == 0, 0.0, spread)
    from_right = jnp.where(lane == lanes - 1, 0.0, spread)
    row = lax.broadcasted_iota(jnp.int32, spread.shape, 0)
    from_below = jnp.where(row == 0, 0.0, spread)
    from_above = jnp.where(row == rows - 1, 0.0, spread)
    keep = 1.0 - 4.0 * spread
    for i in range(cells):
        for c in range(3):
            x = conc_ref[c, i]
            sides = from_left * pltpu.roll(x, 1, 1) + from_right * pltpu.roll(x, lanes - 1, 1)
            ends = from_below * pltpu.roll(x, 1, 0) + from_above * pltpu.roll(x, rows - 1, 0)
            src_ref[c, i] = keep * x + ends + sides
    maps = None
    for i in range(cells):
        src = [src_ref[c, i] for c in range(3)]
        cour = [cour_ref[c, i] for c in range(3)]
        rate = [rate_ref[c, i] for c in range(2)]
        under = [1.0 + cour[0] + rate[0], 1.0 + cour[1] + rate[1], 1.0 + cour[2]]
        pair = under[0] * under[1]
        whole = 1.0 / (pair * under[2])
        both = whole * under[2]
        inv = [both * under[1], both * under[0], whole * pair]
        for c in range(3):
            inv_ref[c, i] = inv[c]
        gain = [cour[c] * inv[c] for c in range(3)]
        if maps is None:
            u0 = inv[0]
            u1 = inv[1] * (rate[0] * u0)
            v1 = inv[1]
            aa = gain[0]
            pa = cour[1] * u1
            pp = gain[1]
            va = gain[2] * (rate[1] * u1)
            vp = gain[2] * (rate[1] * v1)
            vv = gain[2]
            u0 = inv[0] * src[0]
            u1 = inv[1] * (src[1] + rate[0] * u0)
            off_a = cour[0] * u0
            off_p = cour[1] * u1
            off_v = gain[2] * (src[2] + rate[1] * u1)
        else:
            aa, pa, pp, va, vp, vv, off_a, off_p, off_v = maps
            u0 = inv[0] * aa
            u1 = inv[1] * (pa + rate[0] * u0)
            v1 = inv[1] * pp
            aa = cour[0] * u0
            pa = cour[1] * u1
            pp = cour[1] * v1
            va = gain[2] * (va + rate[1] * u1)
            vp = gain[2] * (vp + rate[1] * v1)
            vv = gain[2] * vv
            u0 = inv[0] * (src[0] + off_a)
            u1 = inv[1] * (src[1] + off_p + rate[0] * u0)
            off_a = cour[0] * u0
            off_p = cour[1] * u1
            off_v = gain[2] * (src[2] + off_v + rate[1] * u1)
        maps = (aa, pa, pp, va, vp, vv, off_a, off_p, off_v)
    for j in range(9):
        maps_ref[j] = maps[j]


def seam_kernel(
    across, place_ref, above_ref, below_ref, spread_ref, cour_ref, rate_ref, inv_ref, maps_ref, src_in_ref, src_ref, out_ref
):
    cells, rows = src_ref.shape[1:3]
    side = place_ref[0] % across

    def edge(ref, *index):
        return jnp.concatenate([ref[(*index, pl.ds(0, 8))], ref[(*index, pl.ds(rows - 8, 8))]], axis=0)

    spread = edge(spread_ref)
    line = lax.broadcasted_iota(jnp.int32, spread.shape, 0)
    from_below = jnp.where(jnp.logical_and(line == 0, side > 0), spread, 0.0)
    from_above = jnp.where(jnp.logical_and(line == 15, side < across - 1), spread, 0.0)
    flux = None
    for i in range(cells):
        inv = [edge(inv_ref, c, i) for c in range(3)]
        cour = [edge(cour_ref, c, i) for c in range(3)]
        rate = [edge(rate_ref, c, i) for c in range(2)]
        add = []
        for c in range(3):
            below = below_ref[pl.ds(c * cells + i, 1), :]
            above = above_ref[pl.ds(c * cells + i, 1), :]
            value = from_below * below + from_above * above
            add.append(value)
            src_ref[c, i, pl.ds(0, 8)] = src_in_ref[c, i, pl.ds(0, 8)] + value[:8]
            src_ref[c, i, pl.ds(rows - 8, 8)] = src_in_ref[c, i, pl.ds(rows - 8, 8)] + value[8:]
        if flux is not None:
            add = [add[c] + flux[c] for c in range(3)]
        u0 = inv[0] * add[0]
        u1 = inv[1] * (add[1] + rate[0] * u0)
        u2 = inv[2] * (add[2] + rate[1] * u1)
        flux = [cour[0] * u0, cour[1] * u1, cour[2] * u2]
    listed = [maps_ref[j] for j in range(9)]
    for c in range(3):
        own = listed[6 + c]
        listed[6 + c] = jnp.concatenate(
            [own[:8] + flux[c][:8], own[8:rows - 8], own[rows - 8:] + flux[c][8:]], axis=0
        )
    listed.append(listed[8])
    for j in range(SLOTS):
        first, second = halves(listed[2 * j], listed[2 * j + 1])
        out_ref[pl.ds(j, rows, stride=2 * SLOTS), :] = first
        out_ref[pl.ds(SLOTS + j, rows, stride=2 * SLOTS), :] = second


def relay_kernel(across, place_ref, maps_ref, inlet_ref, out_ref, map_scr, flux_scr):
    count = out_ref.shape[0] // 2
    lanes = out_ref.shape[1]
    half = lanes // 2
    for j in range(5):
        pair = maps_ref[pl.ds(j, count, stride=SLOTS), :]
        map_scr[2 * j] = pair
        if 2 * j + 1 < 9:
            map_scr[2 * j + 1] = pltpu.roll(pair, half, 1)
    place = place_ref[0] // across
    row = place // 2
    odd = place % 2
    flux = []
    for c in range(3):
        line = inlet_ref[c, pl.ds(row, 1), :]
        flux.append(jnp.where(odd == 1, pltpu.roll(line, half, 1), line))
    for f in range(count):
        for c in range(3):
            flux_scr[c, pl.ds(f, 1), :] = flux[c]
        m = [map_scr[j, pl.ds(f, 1), :] for j in range(9)]
        flux = [
            m[0] * flux[0] + m[6],
            (m[1] * flux[0] + m[7]) + m[2] * flux[1],
            (m[3] * flux[0] + m[8]) + (m[4] * flux[1] + m[5] * flux[2]),
        ]
    lane = lax.broadcasted_iota(jnp.int32, (count, lanes), 1)
    first = jnp.where(lane < half, flux_scr[0], pltpu.roll(flux_scr[1], half, 1))
    out_ref[pl.ds(0, count, stride=2), :] = first
    out_ref[pl.ds(1, count, stride=2), :] = flux_scr[2]


def fresh_kernel(flux_ref, src_ref, inv_ref, cour_ref, rate_ref, out_hbm, out_ref, sems):
    cells, rows, lanes = src_ref.shape[1:]
    half = lanes // 2
    lane = lax.broadcasted_iota(jnp.int32, (rows, lanes), 1)

    def half_row(h, j):
        return flux_ref[pl.ds(2 * h + j, rows, stride=4), :]

    pair_l, pair_h = half_row(0, 0), half_row(1, 0)
    third_l, third_h = half_row(0, 1), half_row(1, 1)
    flux = [
        jnp.where(lane < half, pair_l, pltpu.roll(pair_h, half, 1)),
        jnp.where(lane < half, pltpu.roll(pair_l, half, 1), pair_h),
        jnp.where(lane < half, third_l, pltpu.roll(third_h, half, 1)),
    ]
    part = cells // sems.shape[0]
    copies = []
    for i in range(cells):
        first = inv_ref[0, i] * (src_ref[0, i] + flux[0])
        second = inv_ref[1, i] * (src_ref[1, i] + flux[1] + rate_ref[0, i] * first)
        third = inv_ref[2, i] * (src_ref[2, i] + flux[2] + rate_ref[1, i] * second)
        values = (first, second, third)
        for c in range(3):
            out_ref[c, i] = values[c]
        flux = [cour_ref[c, i] * values[c] for c in range(3)]
        if (i + 1) % part == 0:
            span = pl.ds(i + 1 - part, part)
            copies.append(pltpu.make_async_copy(out_ref.at[:, span], out_hbm.at[:, span], sems.at[i // part]))
            copies[-1].start()
    for copy in copies:
        copy.wait()


def per_device(concentration, courant, rates, spread, inlet):
    _, cells, rows, lanes = concentration.shape
    count = lax.axis_size("flow")
    across = lax.axis_size("lat")
    f32 = jnp.float32
    place = (lax.axis_index("flow") * across + lax.axis_index("lat")).reshape(1)
    block = jax.ShapeDtypeStruct(concentration.shape, f32)
    lines = jax.ShapeDtypeStruct((3, cells, lanes), f32)
    hbm = pl.BlockSpec(memory_space=pltpu.HBM)
    conc, low, high, rate, spread, inlet = pl.pallas_call(
        load_kernel,
        out_shape=(
            block,
            lines,
            lines,
            jax.ShapeDtypeStruct(rates.shape, f32),
            jax.ShapeDtypeStruct(spread.shape, f32),
            jax.ShapeDtypeStruct(inlet.shape, f32),
        ),
        in_specs=[hbm] * 4,
        out_specs=(VMEM,) * 6,
        scratch_shapes=[pltpu.SemaphoreType.DMA((6,))],
        compiler_params=PARAMS,
        cost_estimate=pl.CostEstimate(flops=0, bytes_accessed=64 * 1024 * 1024, transcendentals=0),
        name="load",
    )(in_hbm(concentration), in_hbm(rates), in_hbm(spread), in_hbm(inlet))
    ring = [(i, (i + 1) % across) for i in range(across)]
    above = lax.ppermute(low.reshape(3 * cells, lanes), "lat", [(b, a) for a, b in ring])
    below = lax.ppermute(high.reshape(3 * cells, lanes), "lat", ring)
    cour = in_vmem(courant)
    src, inv, maps = pl.pallas_call(
        maps_kernel,
        out_shape=(
            block,
            block,
            jax.ShapeDtypeStruct((9, rows, lanes), f32),
        ),
        in_specs=[VMEM] * 4,
        out_specs=(VMEM,) * 3,
        compiler_params=PARAMS,
        cost_estimate=pl.CostEstimate(flops=0, bytes_accessed=8 * 1024 * 1024, transcendentals=0),
        name="maps",
    )(conc, cour, rate, spread)
    src, packed = pl.pallas_call(
        functools.partial(seam_kernel, across),
        out_shape=(block, jax.ShapeDtypeStruct((count * SLOTS, lanes), f32)),
        in_specs=[SMEM] + [VMEM] * 8,
        out_specs=(VMEM, VMEM),
        input_output_aliases={8: 0},
        compiler_params=PARAMS,
        name="seam",
    )(place, above, below, spread, cour, rate, inv, maps, src)
    packed = lax.all_to_all(packed.reshape(count, SLOTS, 1, lanes), "flow", 0, 0)
    flux = pl.pallas_call(
        functools.partial(relay_kernel, across),
        out_shape=jax.ShapeDtypeStruct((count * 2, lanes), f32),
        in_specs=[SMEM] + [VMEM] * 2,
        out_specs=VMEM,
        scratch_shapes=[pltpu.VMEM((10, count, lanes), f32), pltpu.VMEM((3, count, lanes), f32)],
        compiler_params=PARAMS,
        name="relay",
    )(place, packed.reshape(count * SLOTS, lanes), inlet)
    flux = lax.all_to_all(flux.reshape(count, 2, lanes), "flow", 0, 0)
    return pl.pallas_call(
        fresh_kernel,
        out_shape=block,
        in_specs=[VMEM] * 5,
        out_specs=hbm,
        scratch_shapes=[pltpu.VMEM(block.shape, f32), pltpu.SemaphoreType.DMA((4,))],
        compiler_params=PARAMS,
        name="fresh",
    )(flux.reshape(count * 2, lanes), src, inv, cour, rate)


def solution(mesh):
    in_specs = (
        P(None, "flow", "lat", None),
        P(None, "flow", "lat", None),
        P(None, "flow", "lat", None),
        P("lat", None),
        P(None, "lat", None),
    )
    out_specs = P(None, "flow", "lat", None)
    return jax.shard_map(
        per_device, mesh=mesh, in_specs=in_specs, out_specs=out_specs, check_vma=False
    )
```

```python
import functools

import jax
import jax.numpy as jnp
from jax import lax
from jax.experimental import pallas as pl
from jax.experimental.pallas import tpu as pltpu
from jax.sharding import PartitionSpec as P

VMEM = pl.BlockSpec(memory_space=pltpu.VMEM)
SMEM = pl.BlockSpec(memory_space=pltpu.SMEM)
PARAMS = pltpu.CompilerParams(vmem_limit_bytes=16 * 1024 * 1024)
GROUP = 8
SLOTS = 5


def in_hbm(value):
    return pltpu.with_memory_space_constraint(value, pltpu.HBM)


def in_vmem(value):
    return pltpu.with_memory_space_constraint(value, pltpu.VMEM)


def halves(low, high):
    lane = lax.broadcasted_iota(jnp.int32, low.shape, 1)
    half = low.shape[1] // 2
    first = jnp.where(lane < half, low, pltpu.roll(high, half, 1))
    second = jnp.where(lane < half, pltpu.roll(low, half, 1), high)
    return first, second


def edges_kernel(conc_hbm, low_ref, high_ref, sems):
    rows = conc_hbm.shape[2]
    low_copy = pltpu.make_async_copy(conc_hbm.at[:, :, 0, :], low_ref, sems.at[0])
    high_copy = pltpu.make_async_copy(conc_hbm.at[:, :, rows - 1, :], high_ref, sems.at[1])
    low_copy.start()
    high_copy.start()
    low_copy.wait()
    high_copy.wait()


def pack(out_ref, row, low, high):
    rows = low.shape[0]
    first, second = halves(low, high)
    out_ref[pl.ds(row, rows, stride=2 * SLOTS), :] = first
    out_ref[pl.ds(SLOTS + row, rows, stride=2 * SLOTS), :] = second


def maps_kernel(conc_ref, cour_ref, rate_ref, spread_ref, src_ref, inv_ref, off_ref, out_ref):
    cells = src_ref.shape[1]
    spread = spread_ref[...]
    rows, lanes = spread.shape
    lane = lax.broadcasted_iota(jnp.int32, spread.shape, 1)
    from_left = jnp.where(lane == 0, 0.0, spread)
    from_right = jnp.where(lane == lanes - 1, 0.0, spread)
    row = lax.broadcasted_iota(jnp.int32, spread.shape, 0)
    from_below = jnp.where(row == 0, 0.0, spread)
    from_above = jnp.where(row == rows - 1, 0.0, spread)
    keep = 1.0 - 4.0 * spread
    for i in range(cells):
        for c in range(3):
            x = conc_ref[c, i]
            sides = from_left * pltpu.roll(x, 1, 1) + from_right * pltpu.roll(x, lanes - 1, 1)
            ends = from_below * pltpu.roll(x, 1, 0) + from_above * pltpu.roll(x, rows - 1, 0)
            src_ref[c, i] = keep * x + ends + sides
    maps = None
    for i in range(cells):
        src = [src_ref[c, i] for c in range(3)]
        cour = [cour_ref[c, i] for c in range(3)]
        rate = [rate_ref[c, i] for c in range(2)]
        under = [1.0 + cour[0] + rate[0], 1.0 + cour[1] + rate[1], 1.0 + cour[2]]
        pair = under[0] * under[1]
        whole = 1.0 / (pair * under[2])
        both = whole * under[2]
        inv = [both * under[1], both * under[0], whole * pair]
        for c in range(3):
            inv_ref[c, i] = inv[c]
        gain = [cour[c] * inv[c] for c in range(3)]
        if maps is None:
            u0 = inv[0]
            u1 = inv[1] * (rate[0] * u0)
            v1 = inv[1]
            aa = gain[0]
            pa = cour[1] * u1
            pp = gain[1]
            va = gain[2] * (rate[1] * u1)
            vp = gain[2] * (rate[1] * v1)
            vv = gain[2]
            u0 = inv[0] * src[0]
            u1 = inv[1] * (src[1] + rate[0] * u0)
            off_a = cour[0] * u0
            off_p = cour[1] * u1
            off_v = gain[2] * (src[2] + rate[1] * u1)
        else:
            aa, pa, pp, va, vp, vv, off_a, off_p, off_v = maps
            u0 = inv[0] * aa
            u1 = inv[1] * (pa + rate[0] * u0)
            v1 = inv[1] * pp
            aa = cour[0] * u0
            pa = cour[1] * u1
            pp = cour[1] * v1
            va = gain[2] * (va + rate[1] * u1)
            vp = gain[2] * (vp + rate[1] * v1)
            vv = gain[2] * vv
            u0 = inv[0] * (src[0] + off_a)
            u1 = inv[1] * (src[1] + off_p + rate[0] * u0)
            off_a = cour[0] * u0
            off_p = cour[1] * u1
            off_v = gain[2] * (src[2] + off_v + rate[1] * u1)
        maps = (aa, pa, pp, va, vp, vv, off_a, off_p, off_v)
    for j in range(3):
        pack(out_ref, j, maps[2 * j], maps[2 * j + 1])
        off_ref[j] = maps[6 + j]


def seam_kernel(
    across,
    place_ref,
    above_ref,
    below_ref,
    spread_ref,
    cour_ref,
    rate_ref,
    inv_ref,
    off_ref,
    src_in_ref,
    out_in_ref,
    src_ref,
    out_ref,
):
    del out_in_ref
    cells, rows = src_ref.shape[1:3]
    side = place_ref[0] % across

    def edge(ref, *index):
        return jnp.concatenate([ref[(*index, pl.ds(0, 8))], ref[(*index, pl.ds(rows - 8, 8))]], axis=0)

    spread = edge(spread_ref)
    line = lax.broadcasted_iota(jnp.int32, spread.shape, 0)
    from_below = jnp.where(jnp.logical_and(line == 0, side > 0), spread, 0.0)
    from_above = jnp.where(jnp.logical_and(line == 15, side < across - 1), spread, 0.0)
    flux = None
    for i in range(cells):
        inv = [edge(inv_ref, c, i) for c in range(3)]
        cour = [edge(cour_ref, c, i) for c in range(3)]
        rate = [edge(rate_ref, c, i) for c in range(2)]
        add = []
        for c in range(3):
            below = below_ref[pl.ds(c * cells + i, 1), :]
            above = above_ref[pl.ds(c * cells + i, 1), :]
            value = from_below * below + from_above * above
            add.append(value)
            src_ref[c, i, pl.ds(0, 8)] = src_in_ref[c, i, pl.ds(0, 8)] + value[:8]
            src_ref[c, i, pl.ds(rows - 8, 8)] = src_in_ref[c, i, pl.ds(rows - 8, 8)] + value[8:]
        if flux is not None:
            add = [add[c] + flux[c] for c in range(3)]
        u0 = inv[0] * add[0]
        u1 = inv[1] * (add[1] + rate[0] * u0)
        u2 = inv[2] * (add[2] + rate[1] * u1)
        flux = [cour[0] * u0, cour[1] * u1, cour[2] * u2]
    offset = []
    for c in range(3):
        own = off_ref[c]
        offset.append(
            jnp.concatenate([own[:8] + flux[c][:8], own[8:rows - 8], own[rows - 8:] + flux[c][8:]], axis=0)
        )
    pack(out_ref, 3, offset[0], offset[1])
    pack(out_ref, 4, offset[2], offset[2])


def chained(later, earlier):
    la, pa, pp, va, vp, vv, oa, op, ov = later
    ea, fa, fp, ga, gp, gv, xa, xp, xv = earlier
    return (
        la * ea,
        pa * ea + pp * fa,
        pp * fp,
        (va * ea + vp * fa) + vv * ga,
        vp * fp + vv * gp,
        vv * gv,
        la * xa + oa,
        (pa * xa + op) + pp * xp,
        (va * xa + ov) + (vp * xp + vv * xv),
    )


def applied(m, flux):
    return [
        m[0] * flux[0] + m[6],
        (m[1] * flux[0] + m[7]) + m[2] * flux[1],
        (m[3] * flux[0] + m[8]) + (m[4] * flux[1] + m[5] * flux[2]),
    ]


def relay_kernel(across, place_ref, maps_ref, inlet_ref, out_ref, total_scr, flux_scr):
    lanes = out_ref.shape[1]
    half = lanes // 2
    chains = out_ref.shape[0] // (2 * GROUP)
    before = []
    total = None
    for step in range(GROUP):
        pairs = [maps_ref[pl.ds(step * SLOTS + j, chains, stride=GROUP * SLOTS), :] for j in range(SLOTS)]
        turned = [pltpu.roll(pair, half, 1) for pair in pairs[:-1]]
        one = (
            pairs[0], turned[0], pairs[1], turned[1], pairs[2], turned[2], pairs[3], turned[3], pairs[4]
        )
        before.append(total)
        total = one if total is None else chained(one, total)
    for j in range(9):
        total_scr[j] = total[j]
    place = place_ref[0] // across
    row = place // 2
    odd = place % 2
    flux = []
    for c in range(3):
        line = inlet_ref[c, pl.ds(row, 1), :]
        flux.append(jnp.where(odd == 1, pltpu.roll(line, half, 1), line))
    for chain in range(chains):
        for c in range(3):
            flux_scr[c, pl.ds(chain, 1), :] = flux[c]
        if chain + 1 < chains:
            flux = applied([total_scr[j, pl.ds(chain, 1), :] for j in range(9)], flux)
    heads = [flux_scr[c] for c in range(3)]
    lane = lax.broadcasted_iota(jnp.int32, (chains, lanes), 1)
    for step in range(GROUP):
        flux = heads if step == 0 else applied(before[step], heads)
        first = jnp.where(lane < half, flux[0], pltpu.roll(flux[1], half, 1))
        out_ref[pl.ds(2 * step, chains, stride=2 * GROUP), :] = first
        out_ref[pl.ds(2 * step + 1, chains, stride=2 * GROUP), :] = flux[2]


def fresh_kernel(flux_ref, src_ref, inv_ref, cour_ref, rate_ref, out_hbm, out_ref, sems):
    cells, rows, lanes = src_ref.shape[1:]
    half = lanes // 2
    lane = lax.broadcasted_iota(jnp.int32, (rows, lanes), 1)

    def half_row(h, j):
        return flux_ref[pl.ds(2 * h + j, rows, stride=4), :]

    pair_l, pair_h = half_row(0, 0), half_row(1, 0)
    third_l, third_h = half_row(0, 1), half_row(1, 1)
    flux = [
        jnp.where(lane < half, pair_l, pltpu.roll(pair_h, half, 1)),
        jnp.where(lane < half, pltpu.roll(pair_l, half, 1), pair_h),
        jnp.where(lane < half, third_l, pltpu.roll(third_h, half, 1)),
    ]
    part = cells // sems.shape[0]
    copies = []
    for i in range(cells):
        first = inv_ref[0, i] * (src_ref[0, i] + flux[0])
        second = inv_ref[1, i] * (src_ref[1, i] + flux[1] + rate_ref[0, i] * first)
        third = inv_ref[2, i] * (src_ref[2, i] + flux[2] + rate_ref[1, i] * second)
        values = (first, second, third)
        for c in range(3):
            out_ref[c, i] = values[c]
        flux = [cour_ref[c, i] * values[c] for c in range(3)]
        if (i + 1) % part == 0:
            span = pl.ds(i + 1 - part, part)
            copies.append(pltpu.make_async_copy(out_ref.at[:, span], out_hbm.at[:, span], sems.at[i // part]))
            copies[-1].start()
    for copy in copies:
        copy.wait()


def per_device(concentration, courant, rates, spread, inlet):
    _, cells, rows, lanes = concentration.shape
    count = lax.axis_size("flow")
    across = lax.axis_size("lat")
    f32 = jnp.float32
    place = (lax.axis_index("flow") * across + lax.axis_index("lat")).reshape(1)
    block = jax.ShapeDtypeStruct(concentration.shape, f32)
    lines = jax.ShapeDtypeStruct((3, cells, lanes), f32)
    hbm = pl.BlockSpec(memory_space=pltpu.HBM)
    low, high = pl.pallas_call(
        edges_kernel,
        out_shape=(lines, lines),
        in_specs=[hbm],
        out_specs=(VMEM, VMEM),
        scratch_shapes=[pltpu.SemaphoreType.DMA((2,))],
        compiler_params=PARAMS,
        cost_estimate=pl.CostEstimate(flops=10**11, bytes_accessed=1024, transcendentals=0),
        name="edges",
    )(in_hbm(concentration))
    ring = [(i, (i + 1) % across) for i in range(across)]
    above = lax.ppermute(low.reshape(3 * cells, lanes), "lat", [(b, a) for a, b in ring])
    below = lax.ppermute(high.reshape(3 * cells, lanes), "lat", ring)
    conc, cour, rate = in_vmem(concentration), in_vmem(courant), in_vmem(rates)
    spread = in_vmem(spread)
    table = jax.ShapeDtypeStruct((count * SLOTS, lanes), f32)
    src, inv, offset, packed = pl.pallas_call(
        maps_kernel,
        out_shape=(block, block, jax.ShapeDtypeStruct((3, rows, lanes), f32), table),
        in_specs=[VMEM] * 4,
        out_specs=(VMEM,) * 4,
        compiler_params=PARAMS,
        cost_estimate=pl.CostEstimate(flops=0, bytes_accessed=8 * 1024 * 1024, transcendentals=0),
        name="maps",
    )(conc, cour, rate, spread)
    src, packed = pl.pallas_call(
        functools.partial(seam_kernel, across),
        out_shape=(block, table),
        in_specs=[SMEM] + [VMEM] * 9,
        out_specs=(VMEM, VMEM),
        input_output_aliases={8: 0, 9: 1},
        compiler_params=PARAMS,
        name="seam",
    )(place, above, below, spread, cour, rate, inv, offset, src, packed)
    packed = lax.all_to_all(packed.reshape(count, SLOTS, 1, lanes), "flow", 0, 0)
    flux = pl.pallas_call(
        functools.partial(relay_kernel, across),
        out_shape=jax.ShapeDtypeStruct((count * 2, lanes), f32),
        in_specs=[SMEM] + [VMEM] * 2,
        out_specs=VMEM,
        scratch_shapes=[
            pltpu.VMEM((9, count // GROUP, lanes), f32),
            pltpu.VMEM((3, count // GROUP, lanes), f32),
        ],
        compiler_params=PARAMS,
        name="relay",
    )(place, packed.reshape(count * SLOTS, lanes), in_vmem(inlet))
    flux = lax.all_to_all(flux.reshape(count, 2, lanes), "flow", 0, 0)
    return pl.pallas_call(
        fresh_kernel,
        out_shape=block,
        in_specs=[VMEM] * 5,
        out_specs=hbm,
        scratch_shapes=[pltpu.VMEM(block.shape, f32), pltpu.SemaphoreType.DMA((4,))],
        compiler_params=PARAMS,
        name="fresh",
    )(flux.reshape(count * 2, lanes), src, inv, cour, rate)


def solution(mesh):
    in_specs = (
        P(None, "flow", "lat", None),
        P(None, "flow", "lat", None),
        P(None, "flow", "lat", None),
        P("lat", None),
        P(None, "lat", None),
    )
    out_specs = P(None, "flow", "lat", None)
    return jax.shard_map(
        per_device, mesh=mesh, in_specs=in_specs, out_specs=out_specs, check_vma=False
    )
```

```python
import functools

import jax
import jax.numpy as jnp
from jax import lax
from jax.experimental import pallas as pl
from jax.experimental.pallas import tpu as pltpu
from jax.sharding import PartitionSpec as P

VMEM = pl.BlockSpec(memory_space=pltpu.VMEM)
SMEM = pl.BlockSpec(memory_space=pltpu.SMEM)
PARAMS = pltpu.CompilerParams(vmem_limit_bytes=16 * 1024 * 1024)
GROUP = 8
SLOTS = 9


def in_hbm(value):
    return pltpu.with_memory_space_constraint(value, pltpu.HBM)


def in_vmem(value):
    return pltpu.with_memory_space_constraint(value, pltpu.VMEM)


def edges_kernel(conc_hbm, low_ref, high_ref, sems):
    rows = conc_hbm.shape[2]
    low_copy = pltpu.make_async_copy(conc_hbm.at[:, :, 0, :], low_ref, sems.at[0])
    high_copy = pltpu.make_async_copy(conc_hbm.at[:, :, rows - 1, :], high_ref, sems.at[1])
    low_copy.start()
    high_copy.start()
    low_copy.wait()
    high_copy.wait()


def pack(out_ref, slot, value):
    rows = value.shape[0]
    for team in range(out_ref.shape[0] // (SLOTS * rows)):
        out_ref[pl.ds(team * rows * SLOTS + slot, rows, stride=SLOTS), :] = value


def maps_kernel(conc_ref, cour_ref, rate_ref, spread_ref, src_ref, inv_ref, off_ref, out_ref):
    cells = src_ref.shape[1]
    spread = spread_ref[...]
    rows, lanes = spread.shape
    lane = lax.broadcasted_iota(jnp.int32, spread.shape, 1)
    from_left = jnp.where(lane == 0, 0.0, spread)
    from_right = jnp.where(lane == lanes - 1, 0.0, spread)
    row = lax.broadcasted_iota(jnp.int32, spread.shape, 0)
    from_below = jnp.where(row == 0, 0.0, spread)
    from_above = jnp.where(row == rows - 1, 0.0, spread)
    keep = 1.0 - 4.0 * spread
    for i in range(cells):
        for c in range(3):
            x = conc_ref[c, i]
            sides = from_left * pltpu.roll(x, 1, 1) + from_right * pltpu.roll(x, lanes - 1, 1)
            ends = from_below * pltpu.roll(x, 1, 0) + from_above * pltpu.roll(x, rows - 1, 0)
            src_ref[c, i] = keep * x + ends + sides
    maps = None
    for i in range(cells):
        src = [src_ref[c, i] for c in range(3)]
        cour = [cour_ref[c, i] for c in range(3)]
        rate = [rate_ref[c, i] for c in range(2)]
        under = [1.0 + cour[0] + rate[0], 1.0 + cour[1] + rate[1], 1.0 + cour[2]]
        pair = under[0] * under[1]
        whole = 1.0 / (pair * under[2])
        both = whole * under[2]
        inv = [both * under[1], both * under[0], whole * pair]
        for c in range(3):
            inv_ref[c, i] = inv[c]
        gain = [cour[c] * inv[c] for c in range(3)]
        if maps is None:
            u0 = inv[0]
            u1 = inv[1] * (rate[0] * u0)
            v1 = inv[1]
            aa = gain[0]
            pa = cour[1] * u1
            pp = gain[1]
            va = gain[2] * (rate[1] * u1)
            vp = gain[2] * (rate[1] * v1)
            vv = gain[2]
            u0 = inv[0] * src[0]
            u1 = inv[1] * (src[1] + rate[0] * u0)
            off_a = cour[0] * u0
            off_p = cour[1] * u1
            off_v = gain[2] * (src[2] + rate[1] * u1)
        else:
            aa, pa, pp, va, vp, vv, off_a, off_p, off_v = maps
            u0 = inv[0] * aa
            u1 = inv[1] * (pa + rate[0] * u0)
            v1 = inv[1] * pp
            aa = cour[0] * u0
            pa = cour[1] * u1
            pp = cour[1] * v1
            va = gain[2] * (va + rate[1] * u1)
            vp = gain[2] * (vp + rate[1] * v1)
            vv = gain[2] * vv
            u0 = inv[0] * (src[0] + off_a)
            u1 = inv[1] * (src[1] + off_p + rate[0] * u0)
            off_a = cour[0] * u0
            off_p = cour[1] * u1
            off_v = gain[2] * (src[2] + off_v + rate[1] * u1)
        maps = (aa, pa, pp, va, vp, vv, off_a, off_p, off_v)
    for j in range(6):
        pack(out_ref, j, maps[j])
    for c in range(3):
        off_ref[c] = maps[6 + c]


def seam_kernel(
    across,
    place_ref,
    above_ref,
    below_ref,
    spread_ref,
    cour_ref,
    rate_ref,
    inv_ref,
    off_ref,
    src_in_ref,
    out_in_ref,
    src_ref,
    out_ref,
):
    del out_in_ref
    cells, rows = src_ref.shape[1:3]
    side = place_ref[0] % across

    def edge(ref, *index):
        return jnp.concatenate([ref[(*index, pl.ds(0, 8))], ref[(*index, pl.ds(rows - 8, 8))]], axis=0)

    spread = edge(spread_ref)
    line = lax.broadcasted_iota(jnp.int32, spread.shape, 0)
    from_below = jnp.where(jnp.logical_and(line == 0, side > 0), spread, 0.0)
    from_above = jnp.where(jnp.logical_and(line == 15, side < across - 1), spread, 0.0)
    flux = None
    for i in range(cells):
        inv = [edge(inv_ref, c, i) for c in range(3)]
        cour = [edge(cour_ref, c, i) for c in range(3)]
        rate = [edge(rate_ref, c, i) for c in range(2)]
        add = []
        for c in range(3):
            below = below_ref[pl.ds(c * cells + i, 1), :]
            above = above_ref[pl.ds(c * cells + i, 1), :]
            value = from_below * below + from_above * above
            add.append(value)
            src_ref[c, i, pl.ds(0, 8)] = src_in_ref[c, i, pl.ds(0, 8)] + value[:8]
            src_ref[c, i, pl.ds(rows - 8, 8)] = src_in_ref[c, i, pl.ds(rows - 8, 8)] + value[8:]
        if flux is not None:
            add = [add[c] + flux[c] for c in range(3)]
        u0 = inv[0] * add[0]
        u1 = inv[1] * (add[1] + rate[0] * u0)
        u2 = inv[2] * (add[2] + rate[1] * u1)
        flux = [cour[0] * u0, cour[1] * u1, cour[2] * u2]
    for c in range(3):
        own = off_ref[c]
        total = [own[:8] + flux[c][:8], own[8:rows - 8], own[rows - 8:] + flux[c][8:]]
        pack(out_ref, 6 + c, jnp.concatenate(total, axis=0))


def chained(later, earlier):
    la, pa, pp, va, vp, vv, oa, op, ov = later
    ea, fa, fp, ga, gp, gv, xa, xp, xv = earlier
    return (
        la * ea,
        pa * ea + pp * fa,
        pp * fp,
        (va * ea + vp * fa) + vv * ga,
        vp * fp + vv * gp,
        vv * gv,
        la * xa + oa,
        (pa * xa + op) + pp * xp,
        (va * xa + ov) + (vp * xp + vv * xv),
    )


def applied(m, flux):
    return [
        m[0] * flux[0] + m[6],
        (m[1] * flux[0] + m[7]) + m[2] * flux[1],
        (m[3] * flux[0] + m[8]) + (m[4] * flux[1] + m[5] * flux[2]),
    ]


def relay_kernel(across, place_ref, maps_ref, inlet_ref, out_ref, total_scr, head_scr, flux_scr):
    rows = inlet_ref.shape[1]
    chains = total_scr.shape[1]
    before = []
    total = None
    for step in range(GROUP):
        one = tuple(
            maps_ref[pl.ds(step * SLOTS + j, chains, stride=GROUP * SLOTS), :] for j in range(SLOTS)
        )
        before.append(total)
        total = one if total is None else chained(one, total)
    for j in range(9):
        total_scr[j] = total[j]
    place = place_ref[0] // across
    team = place // rows
    row = place % rows
    flux = [inlet_ref[c, pl.ds(row, 1), :] for c in range(3)]
    for chain in range(chains):
        for c in range(3):
            head_scr[c, pl.ds(chain, 1), :] = flux[c]
        if chain + 1 < chains:
            flux = applied([total_scr[j, pl.ds(chain, 1), :] for j in range(9)], flux)
    heads = [head_scr[c] for c in range(3)]
    for step in range(GROUP):
        flux = heads if step == 0 else applied(before[step], heads)
        for c in range(3):
            flux_scr[pl.ds(3 * step + c, chains, stride=3 * GROUP), :] = flux[c]
    size = out_ref.shape[0]
    out_ref[...] = flux_scr[pl.ds(pl.multiple_of(team * size, 8), size), :]


def fresh_kernel(flux_ref, src_ref, inv_ref, cour_ref, rate_ref, out_hbm, out_ref, sems):
    cells, rows = src_ref.shape[1:3]
    flux = [flux_ref[pl.ds(c, rows, stride=3), :] for c in range(3)]
    part = cells // sems.shape[0]
    copies = []
    for i in range(cells):
        first = inv_ref[0, i] * (src_ref[0, i] + flux[0])
        second = inv_ref[1, i] * (src_ref[1, i] + flux[1] + rate_ref[0, i] * first)
        third = inv_ref[2, i] * (src_ref[2, i] + flux[2] + rate_ref[1, i] * second)
        values = (first, second, third)
        for c in range(3):
            out_ref[c, i] = values[c]
        flux = [cour_ref[c, i] * values[c] for c in range(3)]
        if (i + 1) % part == 0:
            span = pl.ds(i + 1 - part, part)
            copies.append(pltpu.make_async_copy(out_ref.at[:, span], out_hbm.at[:, span], sems.at[i // part]))
            copies[-1].start()
    for copy in copies:
        copy.wait()


def per_device(concentration, courant, rates, spread, inlet):
    _, cells, rows, lanes = concentration.shape
    count = lax.axis_size("flow")
    across = lax.axis_size("lat")
    f32 = jnp.float32
    place = (lax.axis_index("flow") * across + lax.axis_index("lat")).reshape(1)
    block = jax.ShapeDtypeStruct(concentration.shape, f32)
    lines = jax.ShapeDtypeStruct((3, cells, lanes), f32)
    hbm = pl.BlockSpec(memory_space=pltpu.HBM)
    low, high = pl.pallas_call(
        edges_kernel,
        out_shape=(lines, lines),
        in_specs=[hbm],
        out_specs=(VMEM, VMEM),
        scratch_shapes=[pltpu.SemaphoreType.DMA((2,))],
        compiler_params=PARAMS,
        cost_estimate=pl.CostEstimate(flops=10**11, bytes_accessed=1024, transcendentals=0),
        name="edges",
    )(in_hbm(concentration))
    ring = [(i, (i + 1) % across) for i in range(across)]
    above = lax.ppermute(low.reshape(3 * cells, lanes), "lat", [(b, a) for a, b in ring])
    below = lax.ppermute(high.reshape(3 * cells, lanes), "lat", ring)
    conc, cour, rate = in_vmem(concentration), in_vmem(courant), in_vmem(rates)
    spread = in_vmem(spread)
    table = jax.ShapeDtypeStruct((count * SLOTS, lanes), f32)
    src, inv, offset, packed = pl.pallas_call(
        maps_kernel,
        out_shape=(block, block, jax.ShapeDtypeStruct((3, rows, lanes), f32), table),
        in_specs=[VMEM] * 4,
        out_specs=(VMEM,) * 4,
        compiler_params=PARAMS,
        cost_estimate=pl.CostEstimate(flops=0, bytes_accessed=8 * 1024 * 1024, transcendentals=0),
        name="maps",
    )(conc, cour, rate, spread)
    src, packed = pl.pallas_call(
        functools.partial(seam_kernel, across),
        out_shape=(block, table),
        in_specs=[SMEM] + [VMEM] * 9,
        out_specs=(VMEM, VMEM),
        input_output_aliases={8: 0, 9: 1},
        compiler_params=PARAMS,
        name="seam",
    )(place, above, below, spread, cour, rate, inv, offset, src, packed)
    packed = lax.all_to_all(packed.reshape(count, SLOTS, 1, lanes), "flow", 0, 0)
    flux = pl.pallas_call(
        functools.partial(relay_kernel, across),
        out_shape=jax.ShapeDtypeStruct((rows * 3, lanes), f32),
        in_specs=[SMEM] + [VMEM] * 2,
        out_specs=VMEM,
        scratch_shapes=[
            pltpu.VMEM((9, count // GROUP, lanes), f32),
            pltpu.VMEM((3, count // GROUP, lanes), f32),
            pltpu.VMEM((count * 3, lanes), f32),
        ],
        compiler_params=PARAMS,
        name="relay",
    )(place, packed.reshape(count * SLOTS, lanes), in_vmem(inlet))
    teams = [list(range(first, first + rows)) for first in range(0, count, rows)]
    flux = lax.all_to_all(flux.reshape(rows, 3, 1, lanes), "flow", 0, 0, axis_index_groups=teams)
    return pl.pallas_call(
        fresh_kernel,
        out_shape=block,
        in_specs=[VMEM] * 5,
        out_specs=hbm,
        scratch_shapes=[pltpu.VMEM(block.shape, f32), pltpu.SemaphoreType.DMA((4,))],
        compiler_params=PARAMS,
        name="fresh",
    )(flux.reshape(rows * 3, lanes), src, inv, cour, rate)


def solution(mesh):
    in_specs = (
        P(None, "flow", "lat", None),
        P(None, "flow", "lat", None),
        P(None, "flow", "lat", None),
        P("lat", None),
        P(None, "lat", None),
    )
    out_specs = P(None, "flow", "lat", None)
    return jax.shard_map(
        per_device, mesh=mesh, in_specs=in_specs, out_specs=out_specs, check_vma=False
    )
```

```python
import functools

import jax
import jax.numpy as jnp
from jax import lax
from jax.experimental import pallas as pl
from jax.experimental.pallas import tpu as pltpu
from jax.sharding import PartitionSpec as P

VMEM = pl.BlockSpec(memory_space=pltpu.VMEM)
SMEM = pl.BlockSpec(memory_space=pltpu.SMEM)
PARAMS = pltpu.CompilerParams(vmem_limit_bytes=16 * 1024 * 1024)
GROUP = 4
SLOTS = 9


def in_hbm(value):
    return pltpu.with_memory_space_constraint(value, pltpu.HBM)


def in_vmem(value):
    return pltpu.with_memory_space_constraint(value, pltpu.VMEM)


def edges_kernel(conc_hbm, low_ref, high_ref, sems):
    rows = conc_hbm.shape[2]
    low_copy = pltpu.make_async_copy(conc_hbm.at[:, :, 0, :], low_ref, sems.at[0])
    high_copy = pltpu.make_async_copy(conc_hbm.at[:, :, rows - 1, :], high_ref, sems.at[1])
    low_copy.start()
    high_copy.start()
    low_copy.wait()
    high_copy.wait()


def pack(out_ref, slot, value):
    out_ref[pl.ds(slot, value.shape[0], stride=SLOTS), :] = value


def maps_kernel(conc_ref, cour_ref, rate_ref, spread_ref, src_ref, inv_ref, off_ref, out_ref):
    cells = src_ref.shape[1]
    spread = spread_ref[...]
    rows, lanes = spread.shape
    lane = lax.broadcasted_iota(jnp.int32, spread.shape, 1)
    from_left = jnp.where(lane == 0, 0.0, spread)
    from_right = jnp.where(lane == lanes - 1, 0.0, spread)
    row = lax.broadcasted_iota(jnp.int32, spread.shape, 0)
    from_below = jnp.where(row == 0, 0.0, spread)
    from_above = jnp.where(row == rows - 1, 0.0, spread)
    keep = 1.0 - 4.0 * spread
    for i in range(cells):
        for c in range(3):
            x = conc_ref[c, i]
            sides = from_left * pltpu.roll(x, 1, 1) + from_right * pltpu.roll(x, lanes - 1, 1)
            ends = from_below * pltpu.roll(x, 1, 0) + from_above * pltpu.roll(x, rows - 1, 0)
            src_ref[c, i] = keep * x + ends + sides
    maps = None
    for i in range(cells):
        src = [src_ref[c, i] for c in range(3)]
        cour = [cour_ref[c, i] for c in range(3)]
        rate = [rate_ref[c, i] for c in range(2)]
        under = [1.0 + cour[0] + rate[0], 1.0 + cour[1] + rate[1], 1.0 + cour[2]]
        pair = under[0] * under[1]
        whole = 1.0 / (pair * under[2])
        both = whole * under[2]
        inv = [both * under[1], both * under[0], whole * pair]
        for c in range(3):
            inv_ref[c, i] = inv[c]
        gain = [cour[c] * inv[c] for c in range(3)]
        if maps is None:
            u0 = inv[0]
            u1 = inv[1] * (rate[0] * u0)
            v1 = inv[1]
            aa = gain[0]
            pa = cour[1] * u1
            pp = gain[1]
            va = gain[2] * (rate[1] * u1)
            vp = gain[2] * (rate[1] * v1)
            vv = gain[2]
            u0 = inv[0] * src[0]
            u1 = inv[1] * (src[1] + rate[0] * u0)
            off_a = cour[0] * u0
            off_p = cour[1] * u1
            off_v = gain[2] * (src[2] + rate[1] * u1)
        else:
            aa, pa, pp, va, vp, vv, off_a, off_p, off_v = maps
            u0 = inv[0] * aa
            u1 = inv[1] * (pa + rate[0] * u0)
            v1 = inv[1] * pp
            aa = cour[0] * u0
            pa = cour[1] * u1
            pp = cour[1] * v1
            va = gain[2] * (va + rate[1] * u1)
            vp = gain[2] * (vp + rate[1] * v1)
            vv = gain[2] * vv
            u0 = inv[0] * (src[0] + off_a)
            u1 = inv[1] * (src[1] + off_p + rate[0] * u0)
            off_a = cour[0] * u0
            off_p = cour[1] * u1
            off_v = gain[2] * (src[2] + off_v + rate[1] * u1)
        maps = (aa, pa, pp, va, vp, vv, off_a, off_p, off_v)
    for j in range(6):
        pack(out_ref, j, maps[j])
    for c in range(3):
        off_ref[c] = maps[6 + c]


def seam_kernel(
    across,
    place_ref,
    above_ref,
    below_ref,
    spread_ref,
    cour_ref,
    rate_ref,
    inv_ref,
    off_ref,
    src_in_ref,
    out_in_ref,
    src_ref,
    out_ref,
):
    del out_in_ref
    cells, rows = src_ref.shape[1:3]
    side = place_ref[0] % across

    def edge(ref, *index):
        return jnp.concatenate([ref[(*index, pl.ds(0, 8))], ref[(*index, pl.ds(rows - 8, 8))]], axis=0)

    spread = edge(spread_ref)
    line = lax.broadcasted_iota(jnp.int32, spread.shape, 0)
    from_below = jnp.where(jnp.logical_and(line == 0, side > 0), spread, 0.0)
    from_above = jnp.where(jnp.logical_and(line == 15, side < across - 1), spread, 0.0)
    flux = None
    for i in range(cells):
        inv = [edge(inv_ref, c, i) for c in range(3)]
        cour = [edge(cour_ref, c, i) for c in range(3)]
        rate = [edge(rate_ref, c, i) for c in range(2)]
        add = []
        for c in range(3):
            below = below_ref[pl.ds(c * cells + i, 1), :]
            above = above_ref[pl.ds(c * cells + i, 1), :]
            value = from_below * below + from_above * above
            add.append(value)
            src_ref[c, i, pl.ds(0, 8)] = src_in_ref[c, i, pl.ds(0, 8)] + value[:8]
            src_ref[c, i, pl.ds(rows - 8, 8)] = src_in_ref[c, i, pl.ds(rows - 8, 8)] + value[8:]
        if flux is not None:
            add = [add[c] + flux[c] for c in range(3)]
        u0 = inv[0] * add[0]
        u1 = inv[1] * (add[1] + rate[0] * u0)
        u2 = inv[2] * (add[2] + rate[1] * u1)
        flux = [cour[0] * u0, cour[1] * u1, cour[2] * u2]
    for c in range(3):
        own = off_ref[c]
        total = [own[:8] + flux[c][:8], own[8:rows - 8], own[rows - 8:] + flux[c][8:]]
        pack(out_ref, 6 + c, jnp.concatenate(total, axis=0))


def chained(later, earlier):
    la, pa, pp, va, vp, vv, oa, op, ov = later
    ea, fa, fp, ga, gp, gv, xa, xp, xv = earlier
    return (
        la * ea,
        pa * ea + pp * fa,
        pp * fp,
        (va * ea + vp * fa) + vv * ga,
        vp * fp + vv * gp,
        vv * gv,
        la * xa + oa,
        (pa * xa + op) + pp * xp,
        (va * xa + ov) + (vp * xp + vv * xv),
    )


def applied(m, flux):
    return [
        m[0] * flux[0] + m[6],
        (m[1] * flux[0] + m[7]) + m[2] * flux[1],
        (m[3] * flux[0] + m[8]) + (m[4] * flux[1] + m[5] * flux[2]),
    ]


def chains_of(maps_ref, total_scr):
    chains = total_scr.shape[1]
    before = []
    total = None
    for step in range(GROUP):
        one = tuple(
            maps_ref[pl.ds(step * SLOTS + j, chains, stride=GROUP * SLOTS), :] for j in range(SLOTS)
        )
        before.append(total)
        total = one if total is None else chained(one, total)
    for j in range(9):
        total_scr[j] = total[j]
    return before


def chain_at(total_scr, chain):
    return [total_scr[j, pl.ds(chain, 1), :] for j in range(9)]


def own_row(across, place_ref, inlet_ref):
    rows = inlet_ref.shape[1]
    row = (place_ref[0] // across) % rows
    return [inlet_ref[c, pl.ds(row, 1), :] for c in range(3)]


def middle_kernel(across, place_ref, maps_ref, inlet_ref, out_ref, total_scr):
    chains_of(maps_ref, total_scr)
    flux = own_row(across, place_ref, inlet_ref)
    for chain in range(total_scr.shape[1]):
        flux = applied(chain_at(total_scr, chain), flux)
    for c in range(3):
        out_ref[pl.ds(c, 1), :] = flux[c]


def relay_kernel(across, place_ref, maps_ref, inlet_ref, middle_ref, out_ref, total_scr, head_scr):
    chains = total_scr.shape[1]
    before = chains_of(maps_ref, total_scr)
    leading = place_ref[0] // across < inlet_ref.shape[1]
    inlet = own_row(across, place_ref, inlet_ref)
    flux = [jnp.where(leading, inlet[c], middle_ref[pl.ds(c, 1), :]) for c in range(3)]
    shift = jnp.where(leading, 0, chains // 2)
    for step in range(chains):
        chain = (step + shift) % chains
        for c in range(3):
            head_scr[c, pl.ds(chain, 1), :] = flux[c]
        if step + 1 < chains:
            flux = applied(chain_at(total_scr, chain), flux)
    heads = [head_scr[c] for c in range(3)]
    for step in range(GROUP):
        flux = heads if step == 0 else applied(before[step], heads)
        for c in range(3):
            out_ref[pl.ds(3 * step + c, chains, stride=3 * GROUP), :] = flux[c]


def fresh_kernel(flux_ref, src_ref, inv_ref, cour_ref, rate_ref, out_hbm, out_ref, sems):
    cells, rows = src_ref.shape[1:3]
    flux = [flux_ref[pl.ds(c, rows, stride=3), :] for c in range(3)]
    part = cells // sems.shape[0]
    copies = []
    for i in range(cells):
        first = inv_ref[0, i] * (src_ref[0, i] + flux[0])
        second = inv_ref[1, i] * (src_ref[1, i] + flux[1] + rate_ref[0, i] * first)
        third = inv_ref[2, i] * (src_ref[2, i] + flux[2] + rate_ref[1, i] * second)
        values = (first, second, third)
        for c in range(3):
            out_ref[c, i] = values[c]
        flux = [cour_ref[c, i] * values[c] for c in range(3)]
        if (i + 1) % part == 0:
            span = pl.ds(i + 1 - part, part)
            copies.append(pltpu.make_async_copy(out_ref.at[:, span], out_hbm.at[:, span], sems.at[i // part]))
            copies[-1].start()
    for copy in copies:
        copy.wait()


def per_device(concentration, courant, rates, spread, inlet):
    _, cells, rows, lanes = concentration.shape
    count = lax.axis_size("flow")
    across = lax.axis_size("lat")
    f32 = jnp.float32
    place = (lax.axis_index("flow") * across + lax.axis_index("lat")).reshape(1)
    block = jax.ShapeDtypeStruct(concentration.shape, f32)
    lines = jax.ShapeDtypeStruct((3, cells, lanes), f32)
    hbm = pl.BlockSpec(memory_space=pltpu.HBM)
    low, high = pl.pallas_call(
        edges_kernel,
        out_shape=(lines, lines),
        in_specs=[hbm],
        out_specs=(VMEM, VMEM),
        scratch_shapes=[pltpu.SemaphoreType.DMA((2,))],
        compiler_params=PARAMS,
        cost_estimate=pl.CostEstimate(flops=10**11, bytes_accessed=1024, transcendentals=0),
        name="edges",
    )(in_hbm(concentration))
    ring = [(i, (i + 1) % across) for i in range(across)]
    above = lax.ppermute(low.reshape(3 * cells, lanes), "lat", [(b, a) for a, b in ring])
    below = lax.ppermute(high.reshape(3 * cells, lanes), "lat", ring)
    conc, cour, rate = in_vmem(concentration), in_vmem(courant), in_vmem(rates)
    spread = in_vmem(spread)
    table = jax.ShapeDtypeStruct((rows * SLOTS, lanes), f32)
    src, inv, offset, packed = pl.pallas_call(
        maps_kernel,
        out_shape=(block, block, jax.ShapeDtypeStruct((3, rows, lanes), f32), table),
        in_specs=[VMEM] * 4,
        out_specs=(VMEM,) * 4,
        compiler_params=PARAMS,
        cost_estimate=pl.CostEstimate(flops=0, bytes_accessed=8 * 1024 * 1024, transcendentals=0),
        name="maps",
    )(conc, cour, rate, spread)
    src, packed = pl.pallas_call(
        functools.partial(seam_kernel, across),
        out_shape=(block, table),
        in_specs=[SMEM] + [VMEM] * 9,
        out_specs=(VMEM, VMEM),
        input_output_aliases={8: 0, 9: 1},
        compiler_params=PARAMS,
        name="seam",
    )(place, above, below, spread, cour, rate, inv, offset, src, packed)
    assert count == 2 * rows
    middle = rows + rows // 2
    teams = [list(range(rows)), [*range(middle, count), *range(rows, middle)]]
    packed = lax.all_to_all(packed.reshape(rows, SLOTS, 1, lanes), "flow", 0, 0, axis_index_groups=teams)
    packed = packed.reshape(rows * SLOTS, lanes)
    inlet = in_vmem(inlet)
    totals = pltpu.VMEM((9, rows // GROUP, lanes), f32)
    middle = pl.pallas_call(
        functools.partial(middle_kernel, across),
        out_shape=jax.ShapeDtypeStruct((3, lanes), f32),
        in_specs=[SMEM] + [VMEM] * 2,
        out_specs=VMEM,
        scratch_shapes=[totals],
        compiler_params=PARAMS,
        name="middle",
    )(place, packed, inlet)
    middle = lax.ppermute(middle, "flow", list(zip(*teams)))
    flux = pl.pallas_call(
        functools.partial(relay_kernel, across),
        out_shape=jax.ShapeDtypeStruct((rows * 3, lanes), f32),
        in_specs=[SMEM] + [VMEM] * 3,
        out_specs=VMEM,
        scratch_shapes=[totals, pltpu.VMEM((3, rows // GROUP, lanes), f32)],
        compiler_params=PARAMS,
        name="relay",
    )(place, packed, inlet, middle)
    flux = lax.all_to_all(flux.reshape(rows, 3, 1, lanes), "flow", 0, 0, axis_index_groups=teams)
    return pl.pallas_call(
        fresh_kernel,
        out_shape=block,
        in_specs=[VMEM] * 5,
        out_specs=hbm,
        scratch_shapes=[pltpu.VMEM(block.shape, f32), pltpu.SemaphoreType.DMA((4,))],
        compiler_params=PARAMS,
        name="fresh",
    )(flux.reshape(rows * 3, lanes), src, inv, cour, rate)


def solution(mesh):
    in_specs = (
        P(None, "flow", "lat", None),
        P(None, "flow", "lat", None),
        P(None, "flow", "lat", None),
        P("lat", None),
        P(None, "lat", None),
    )
    out_specs = P(None, "flow", "lat", None)
    return jax.shard_map(
        per_device, mesh=mesh, in_specs=in_specs, out_specs=out_specs, check_vma=False
    )
```

```python
import functools

import jax
import jax.numpy as jnp
from jax import lax
from jax.experimental import pallas as pl
from jax.experimental.pallas import tpu as pltpu
from jax.sharding import PartitionSpec as P

VMEM = pl.BlockSpec(memory_space=pltpu.VMEM)
SMEM = pl.BlockSpec(memory_space=pltpu.SMEM)
PARAMS = pltpu.CompilerParams(vmem_limit_bytes=16 * 1024 * 1024)
GROUP = 4
SLOTS = 9


def in_hbm(value):
    return pltpu.with_memory_space_constraint(value, pltpu.HBM)


def in_vmem(value):
    return pltpu.with_memory_space_constraint(value, pltpu.VMEM)


def edges_kernel(conc_hbm, low_ref, high_ref, sems):
    rows = conc_hbm.shape[2]
    copies = []
    for c in range(3):
        copies.append(pltpu.make_async_copy(conc_hbm.at[c, :, rows - 1, :], high_ref.at[c], sems.at[0, c]))
        copies.append(pltpu.make_async_copy(conc_hbm.at[c, :, 0, :], low_ref.at[c], sems.at[1, c]))
    for copy in copies:
        copy.start()
    for copy in copies:
        copy.wait()


def pack(out_ref, slot, value):
    out_ref[pl.ds(slot, value.shape[0], stride=SLOTS), :] = value


def maps_kernel(conc_ref, cour_ref, rate_ref, spread_ref, src_ref, inv_ref, off_ref, out_ref):
    cells = src_ref.shape[1]
    spread = spread_ref[...]
    rows, lanes = spread.shape
    lane = lax.broadcasted_iota(jnp.int32, spread.shape, 1)
    from_left = jnp.where(lane == 0, 0.0, spread)
    from_right = jnp.where(lane == lanes - 1, 0.0, spread)
    row = lax.broadcasted_iota(jnp.int32, spread.shape, 0)
    from_below = jnp.where(row == 0, 0.0, spread)
    from_above = jnp.where(row == rows - 1, 0.0, spread)
    keep = 1.0 - 4.0 * spread
    for i in range(cells):
        for c in range(3):
            x = conc_ref[c, i]
            sides = from_left * pltpu.roll(x, 1, 1) + from_right * pltpu.roll(x, lanes - 1, 1)
            ends = from_below * pltpu.roll(x, 1, 0) + from_above * pltpu.roll(x, rows - 1, 0)
            src_ref[c, i] = keep * x + ends + sides
    maps = None
    for i in range(cells):
        src = [src_ref[c, i] for c in range(3)]
        cour = [cour_ref[c, i] for c in range(3)]
        rate = [rate_ref[c, i] for c in range(2)]
        under = [1.0 + cour[0] + rate[0], 1.0 + cour[1] + rate[1], 1.0 + cour[2]]
        pair = under[0] * under[1]
        whole = 1.0 / (pair * under[2])
        both = whole * under[2]
        inv = [both * under[1], both * under[0], whole * pair]
        for c in range(3):
            inv_ref[c, i] = inv[c]
        gain = [cour[c] * inv[c] for c in range(3)]
        if maps is None:
            u0 = inv[0]
            u1 = inv[1] * (rate[0] * u0)
            v1 = inv[1]
            aa = gain[0]
            pa = cour[1] * u1
            pp = gain[1]
            va = gain[2] * (rate[1] * u1)
            vp = gain[2] * (rate[1] * v1)
            vv = gain[2]
            u0 = inv[0] * src[0]
            u1 = inv[1] * (src[1] + rate[0] * u0)
            off_a = cour[0] * u0
            off_p = cour[1] * u1
            off_v = gain[2] * (src[2] + rate[1] * u1)
        else:
            aa, pa, pp, va, vp, vv, off_a, off_p, off_v = maps
            u0 = inv[0] * aa
            u1 = inv[1] * (pa + rate[0] * u0)
            v1 = inv[1] * pp
            aa = cour[0] * u0
            pa = cour[1] * u1
            pp = cour[1] * v1
            va = gain[2] * (va + rate[1] * u1)
            vp = gain[2] * (vp + rate[1] * v1)
            vv = gain[2] * vv
            u0 = inv[0] * (src[0] + off_a)
            u1 = inv[1] * (src[1] + off_p + rate[0] * u0)
            off_a = cour[0] * u0
            off_p = cour[1] * u1
            off_v = gain[2] * (src[2] + off_v + rate[1] * u1)
        maps = (aa, pa, pp, va, vp, vv, off_a, off_p, off_v)
    for j in range(6):
        pack(out_ref, j, maps[j])
    for c in range(3):
        off_ref[c] = maps[6 + c]


def seam_kernel(
    across,
    place_ref,
    above_ref,
    below_ref,
    spread_ref,
    cour_ref,
    rate_ref,
    inv_ref,
    off_ref,
    src_in_ref,
    out_in_ref,
    src_ref,
    out_ref,
):
    del out_in_ref
    cells, rows = src_ref.shape[1:3]
    side = place_ref[0] % across

    def edge(ref, *index):
        return jnp.concatenate([ref[(*index, pl.ds(0, 8))], ref[(*index, pl.ds(rows - 8, 8))]], axis=0)

    spread = edge(spread_ref)
    line = lax.broadcasted_iota(jnp.int32, spread.shape, 0)
    from_below = jnp.where(jnp.logical_and(line == 0, side > 0), spread, 0.0)
    from_above = jnp.where(jnp.logical_and(line == 15, side < across - 1), spread, 0.0)
    flux = None
    for i in range(cells):
        inv = [edge(inv_ref, c, i) for c in range(3)]
        cour = [edge(cour_ref, c, i) for c in range(3)]
        rate = [edge(rate_ref, c, i) for c in range(2)]
        add = []
        for c in range(3):
            below = below_ref[pl.ds(c * cells + i, 1), :]
            above = above_ref[pl.ds(c * cells + i, 1), :]
            value = from_below * below + from_above * above
            add.append(value)
            src_ref[c, i, pl.ds(0, 8)] = src_in_ref[c, i, pl.ds(0, 8)] + value[:8]
            src_ref[c, i, pl.ds(rows - 8, 8)] = src_in_ref[c, i, pl.ds(rows - 8, 8)] + value[8:]
        if flux is not None:
            add = [add[c] + flux[c] for c in range(3)]
        u0 = inv[0] * add[0]
        u1 = inv[1] * (add[1] + rate[0] * u0)
        u2 = inv[2] * (add[2] + rate[1] * u1)
        flux = [cour[0] * u0, cour[1] * u1, cour[2] * u2]
    for c in range(3):
        own = off_ref[c]
        total = [own[:8] + flux[c][:8], own[8:rows - 8], own[rows - 8:] + flux[c][8:]]
        pack(out_ref, 6 + c, jnp.concatenate(total, axis=0))


def chained(later, earlier):
    la, pa, pp, va, vp, vv, oa, op, ov = later
    ea, fa, fp, ga, gp, gv, xa, xp, xv = earlier
    return (
        la * ea,
        pa * ea + pp * fa,
        pp * fp,
        (va * ea + vp * fa) + vv * ga,
        vp * fp + vv * gp,
        vv * gv,
        la * xa + oa,
        (pa * xa + op) + pp * xp,
        (va * xa + ov) + (vp * xp + vv * xv),
    )


def applied(m, flux):
    return [
        m[0] * flux[0] + m[6],
        (m[1] * flux[0] + m[7]) + m[2] * flux[1],
        (m[3] * flux[0] + m[8]) + (m[4] * flux[1] + m[5] * flux[2]),
    ]


def chains_of(maps_ref, total_scr):
    chains = total_scr.shape[1]
    before = []
    total = None
    for step in range(GROUP):
        one = tuple(
            maps_ref[pl.ds(step * SLOTS + j, chains, stride=GROUP * SLOTS), :] for j in range(SLOTS)
        )
        before.append(total)
        total = one if total is None else chained(one, total)
    for j in range(9):
        total_scr[j] = total[j]
    return before


def chain_at(total_scr, chain):
    return [total_scr[j, pl.ds(chain, 1), :] for j in range(9)]


def own_row(across, place_ref, inlet_ref):
    rows = inlet_ref.shape[1]
    row = (place_ref[0] // across) % rows
    return [inlet_ref[c, pl.ds(row, 1), :] for c in range(3)]


def middle_kernel(across, place_ref, maps_ref, inlet_ref, out_ref, total_scr):
    chains_of(maps_ref, total_scr)
    flux = own_row(across, place_ref, inlet_ref)
    for chain in range(total_scr.shape[1]):
        flux = applied(chain_at(total_scr, chain), flux)
    for c in range(3):
        out_ref[pl.ds(c, 1), :] = flux[c]


def relay_kernel(across, place_ref, maps_ref, inlet_ref, middle_ref, out_ref, total_scr, head_scr):
    chains = total_scr.shape[1]
    before = chains_of(maps_ref, total_scr)
    leading = place_ref[0] // across < inlet_ref.shape[1]
    inlet = own_row(across, place_ref, inlet_ref)
    flux = [jnp.where(leading, inlet[c], middle_ref[pl.ds(c, 1), :]) for c in range(3)]
    shift = jnp.where(leading, 0, chains // 2)
    for step in range(chains):
        chain = (step + shift) % chains
        for c in range(3):
            head_scr[c, pl.ds(chain, 1), :] = flux[c]
        if step + 1 < chains:
            flux = applied(chain_at(total_scr, chain), flux)
    heads = [head_scr[c] for c in range(3)]
    for step in range(GROUP):
        flux = heads if step == 0 else applied(before[step], heads)
        for c in range(3):
            out_ref[pl.ds(3 * step + c, chains, stride=3 * GROUP), :] = flux[c]


def fresh_kernel(flux_ref, src_ref, inv_ref, cour_ref, rate_ref, out_hbm, out_ref, sems):
    cells, rows = src_ref.shape[1:3]
    flux = [flux_ref[pl.ds(c, rows, stride=3), :] for c in range(3)]
    part = cells // sems.shape[0]
    copies = []
    for i in range(cells):
        first = inv_ref[0, i] * (src_ref[0, i] + flux[0])
        second = inv_ref[1, i] * (src_ref[1, i] + flux[1] + rate_ref[0, i] * first)
        third = inv_ref[2, i] * (src_ref[2, i] + flux[2] + rate_ref[1, i] * second)
        values = (first, second, third)
        for c in range(3):
            out_ref[c, i] = values[c]
        flux = [cour_ref[c, i] * values[c] for c in range(3)]
        if (i + 1) % part == 0:
            span = pl.ds(i + 1 - part, part)
            copies.append(pltpu.make_async_copy(out_ref.at[:, span], out_hbm.at[:, span], sems.at[i // part]))
            copies[-1].start()
    for copy in copies:
        copy.wait()


def per_device(concentration, courant, rates, spread, inlet):
    _, cells, rows, lanes = concentration.shape
    count = lax.axis_size("flow")
    across = lax.axis_size("lat")
    f32 = jnp.float32
    place = (lax.axis_index("flow") * across + lax.axis_index("lat")).reshape(1)
    block = jax.ShapeDtypeStruct(concentration.shape, f32)
    lines = jax.ShapeDtypeStruct((3, cells, lanes), f32)
    hbm = pl.BlockSpec(memory_space=pltpu.HBM)
    low, high = pl.pallas_call(
        edges_kernel,
        out_shape=(lines, lines),
        in_specs=[hbm],
        out_specs=(VMEM, VMEM),
        scratch_shapes=[pltpu.SemaphoreType.DMA((2, 3))],
        compiler_params=PARAMS,
        cost_estimate=pl.CostEstimate(flops=10**11, bytes_accessed=1024, transcendentals=0),
        name="edges",
    )(in_hbm(concentration))
    ring = [(i, (i + 1) % across) for i in range(across)]
    above = lax.ppermute(low.reshape(3 * cells, lanes), "lat", [(b, a) for a, b in ring])
    below = lax.ppermute(high.reshape(3 * cells, lanes), "lat", ring)
    conc, cour, rate = in_vmem(concentration), in_vmem(courant), in_vmem(rates)
    spread = in_vmem(spread)
    table = jax.ShapeDtypeStruct((rows * SLOTS, lanes), f32)
    src, inv, offset, packed = pl.pallas_call(
        maps_kernel,
        out_shape=(block, block, jax.ShapeDtypeStruct((3, rows, lanes), f32), table),
        in_specs=[VMEM] * 4,
        out_specs=(VMEM,) * 4,
        compiler_params=PARAMS,
        cost_estimate=pl.CostEstimate(flops=0, bytes_accessed=8 * 1024 * 1024, transcendentals=0),
        name="maps",
    )(conc, cour, rate, spread)
    src, packed = pl.pallas_call(
        functools.partial(seam_kernel, across),
        out_shape=(block, table),
        in_specs=[SMEM] + [VMEM] * 9,
        out_specs=(VMEM, VMEM),
        input_output_aliases={8: 0, 9: 1},
        compiler_params=PARAMS,
        name="seam",
    )(place, above, below, spread, cour, rate, inv, offset, src, packed)
    assert count == 2 * rows
    middle = rows + rows // 2
    teams = [list(range(rows)), [*range(middle, count), *range(rows, middle)]]
    packed = lax.all_to_all(packed.reshape(rows, SLOTS, 1, lanes), "flow", 0, 0, axis_index_groups=teams)
    packed = packed.reshape(rows * SLOTS, lanes)
    inlet = in_vmem(inlet)
    totals = pltpu.VMEM((9, rows // GROUP, lanes), f32)
    middle = pl.pallas_call(
        functools.partial(middle_kernel, across),
        out_shape=jax.ShapeDtypeStruct((3, lanes), f32),
        in_specs=[SMEM] + [VMEM] * 2,
        out_specs=VMEM,
        scratch_shapes=[totals],
        compiler_params=PARAMS,
        name="middle",
    )(place, packed, inlet)
    middle = lax.ppermute(middle, "flow", list(zip(*teams)))
    flux = pl.pallas_call(
        functools.partial(relay_kernel, across),
        out_shape=jax.ShapeDtypeStruct((rows * 3, lanes), f32),
        in_specs=[SMEM] + [VMEM] * 3,
        out_specs=VMEM,
        scratch_shapes=[totals, pltpu.VMEM((3, rows // GROUP, lanes), f32)],
        compiler_params=PARAMS,
        name="relay",
    )(place, packed, inlet, middle)
    flux = lax.all_to_all(flux.reshape(rows, 3, 1, lanes), "flow", 0, 0, axis_index_groups=teams)
    return pl.pallas_call(
        fresh_kernel,
        out_shape=block,
        in_specs=[VMEM] * 5,
        out_specs=hbm,
        scratch_shapes=[pltpu.VMEM(block.shape, f32), pltpu.SemaphoreType.DMA((4,))],
        compiler_params=PARAMS,
        name="fresh",
    )(flux.reshape(rows * 3, lanes), src, inv, cour, rate)


def solution(mesh):
    in_specs = (
        P(None, "flow", "lat", None),
        P(None, "flow", "lat", None),
        P(None, "flow", "lat", None),
        P("lat", None),
        P(None, "lat", None),
    )
    out_specs = P(None, "flow", "lat", None)
    return jax.shard_map(
        per_device, mesh=mesh, in_specs=in_specs, out_specs=out_specs, check_vma=False
    )
```
